32 devices in a mesh: section: 2 (over core), tile: 4 (over z), mem: 4 (over y, x).
Axes of the slice: x: 2, y: 2, z: 4, core: 2. Of those that a mesh axis runs over, the one named last changes fastest.
Arguments:
- state: float32 [32, 16, 64, 128], P(('section', 'mem'), None, 'tile'), may hold values from -6 to 6
- speed_x: float32 [16, 64, 128], P(None, 'tile'), may hold values from -0.35 to 0.35
- speed_y: float32 [16, 64, 128], P(None, 'tile'), may hold values from -0.35 to 0.35
- diffuse: float32 [64, 128], P('tile'), may hold values from 0.02 to 0.07
- obs_cell: int32 [4096], P('tile'), may hold values from 0 to 32767, as said below
- obs_value: float32 [4096], P('tile'), may hold values from -6 to 6
- obs_errinv: float32 [4096], P('tile'), may hold values from 0.05 to 0.5
- obs_list: int32 [32, 64, 256], P('tile'), may hold values from 0 to 3071, as said below
- obs_count: int32 [32, 64], P('tile'), may hold values from 1 to 256, as said below
Outputs:
- analysis: float32 [32, 16, 64, 128], P(('section', 'mem'), None, 'tile')
The draws below stay inside these ranges and needn't reach their ends.
Inputs may be any that keep to these rules, and one draw needn't show every extreme that they name: `obs_cell`: level * 16 * 128 + x * 128 + y of the observation inside its tile. `obs_list`: each row holds 256 different window indices k * 1024 + i, meaning observation i of the tile k - 1 places after the domain's tile; they list window columns nearest first by horizontal distance to the domain's centre; columns beyond 4 * 4 cells and columns outside the grid count as equally far, and ties go by increasing window index, so list tails near the grid's ends may name columns outside it. Only the first obs_count slots of a domain's list are used; away from a few domains, obs_count does not exceed the number of window observations within 2.5 * 4 cells of the centre.
All inputs are finite; a program needn't handle non-finite values.
Results may differ from the reference program's by a relative error of at most 0.0003.
Values sent between devices are 32-bit elements; how exact they have to be, the bound alone decides.
No kernel may reach another device: no remote copies, remote signals or barrier semaphores. Data moves between devices by JAX's collectives and lax.ppermute only.
A program may use at most 64 MiB of HBM per device.

```python
import math
import jax
import jax.numpy as jnp
from jax import lax

ENSEMBLE_SIZE = 32
LEVELS = 16
TILE_CELLS_X = 16
CY = 128
STEPS = 4
DB = 2
OBS_T = 1024
MAXOBS = 256
NX = 64
NOBS = 4096
LOC = 4
N_TILE = 4


def obs_layout(key):
    cells = jax.random.randint(jax.random.fold_in(key, 11), (NOBS,), 0, LEVELS * TILE_CELLS_X * CY, dtype=jnp.int32)
    tiles = jnp.arange(NOBS, dtype=jnp.int32) // OBS_T
    coord_x = tiles * TILE_CELLS_X + cells // CY % TILE_CELLS_X
    coord_y = cells % CY
    valid = jnp.ones((NOBS,), jnp.int32)
    pad_x = jnp.pad(coord_x, (OBS_T, OBS_T))
    pad_y = jnp.pad(coord_y, (OBS_T, OBS_T))
    pad_v = jnp.pad(valid, (OBS_T, OBS_T))
    width = 3 * OBS_T
    limit = 8 * LOC * (8 * LOC)
    cutoff = 5 * LOC * (5 * LOC)
    columns = jnp.arange(width, dtype=jnp.int32)
    centre_y = 2 * DB * jnp.arange(CY // DB, dtype=jnp.int32) + (DB - 1)

    def one_row(row_idx):
        tile_index = row_idx * DB // TILE_CELLS_X
        start = tile_index * OBS_T
        win_x = lax.dynamic_slice_in_dim(pad_x, start, width, 0)
        win_y = lax.dynamic_slice_in_dim(pad_y, start, width, 0)
        win_v = lax.dynamic_slice_in_dim(pad_v, start, width, 0)
        centre_x = 2 * DB * row_idx + (DB - 1)
        delta_x = 2 * win_x - centre_x
        delta_y = 2 * win_y[None, :] - centre_y[:, None]
        dist = delta_x[None, :] * delta_x[None, :] + delta_y * delta_y
        dist = jnp.where(win_v[None, :] > 0, jnp.minimum(dist, limit), limit)
        score = dist * width + columns[None, :]
        picked = lax.top_k(-score, MAXOBS)[1].astype(jnp.int32)
        inside = jnp.sum((dist <= cutoff).astype(jnp.int32), axis=-1)
        return (picked, inside)
    lists, inside = lax.map(one_row, jnp.arange(NX // DB, dtype=jnp.int32))
    return (cells, lists, inside)


def draw_obs_cell(key, part):
    return obs_layout(key)[0]


def draw_obs_list(key, part):
    return obs_layout(key)[1]


def draw_obs_count(key, part):
    inside = obs_layout(key)[2]
    wished = jax.random.randint(jax.random.fold_in(key, 13), inside.shape, 1, MAXOBS + 1, dtype=jnp.int32)
    counts = jnp.minimum(wished, jnp.maximum(inside, 1))
    flattened_state = counts.reshape(-1)
    middle = NX // DB // 2 * (CY // DB) + CY // DB // 2
    flattened_state = flattened_state.at[0].set(1)
    flattened_state = flattened_state.at[middle].set(MAXOBS)
    return flattened_state.reshape(inside.shape)


def block_levels(own_key, extent, shards, low, high):
    gain, own = 1.0, jax.random.fold_in(own_key, 6)
    for axis_at, parts in shards:
        steps = jnp.exp(jax.random.uniform(jax.random.fold_in(own, axis_at), (parts,), jnp.float32, low / len(shards), high / len(shards)))
        gain = gain * jnp.repeat(steps, extent[axis_at] // parts).reshape([-1 if axis == axis_at else 1 for axis in range(len(extent))])
    return gain


def noise(own_key, extent, scale, most, pieces=(), kind=jnp.bfloat16):
    factor_of = block_levels(own_key, extent, pieces, -0.22, 0.18) if pieces else 1.0
    values = jax.random.normal(own_key, extent, jnp.float32) * scale * factor_of
    return jnp.minimum(jnp.maximum(values, -most), most).astype(kind)


def setup_inputs(seed: int = 0) -> dict:
    keys = jax.random.split(jax.random.key(seed), 10)
    state = noise(keys[0], (ENSEMBLE_SIZE, LEVELS, NX, CY), 1.0, 6.0, ((0, 8), (2, 4)), jnp.float32)
    speed_x = jnp.clip(jax.random.uniform(keys[1], (LEVELS, NX, CY), jnp.float32, -0.35, 0.35) * block_levels(keys[1], (LEVELS, NX, CY), ((1, 4),), -0.4, 0.0), -0.35, 0.35)
    speed_y = jnp.clip(jax.random.uniform(keys[2], (LEVELS, NX, CY), jnp.float32, -0.35, 0.35) * block_levels(keys[2], (LEVELS, NX, CY), ((1, 4),), -0.4, 0.0), -0.35, 0.35)
    diffuse = jnp.clip(jnp.exp(math.log(0.07) - 1.252763 * jax.random.uniform(keys[3], (NX, CY), jnp.float32) ** block_levels(keys[3], (NX, CY), ((0, 4),), -0.2, 0.2)), 0.02, 0.07)
    obs_cell = draw_obs_cell(jax.random.fold_in(keys[9], 71), 0)
    obs_value = noise(keys[5], (NOBS,), 1.0, 6.0, ((0, 4),), jnp.float32)
    obs_errinv = jnp.clip(jnp.exp(math.log(0.5) - 2.3025851 * jax.random.uniform(keys[6], (NOBS,), jnp.float32) ** block_levels(keys[6], (NOBS,), ((0, 4),), -0.2, 0.2)), 0.05, 0.5)
    obs_list = draw_obs_list(jax.random.fold_in(keys[9], 71), 0)
    obs_count = draw_obs_count(jax.random.fold_in(keys[9], 71), 0)
    return {"state": state, "speed_x": speed_x, "speed_y": speed_y, "diffuse": diffuse, "obs_cell": obs_cell, "obs_value": obs_value, "obs_errinv": obs_errinv, "obs_list": obs_list, "obs_count": obs_count}


def advance(center, left_x, right_x, speed_x, speed_y, diffuse):
    zero_col = jnp.zeros_like(center[..., :1])
    lower_y = jnp.concatenate([zero_col, center[..., :-1]], axis=-1)
    upper_y = jnp.concatenate([center[..., 1:], zero_col], axis=-1)
    return center - jnp.maximum(speed_x, 0.0) * (center - left_x) - jnp.minimum(speed_x, 0.0) * (right_x - center) - jnp.maximum(speed_y, 0.0) * (center - lower_y) - jnp.minimum(speed_y, 0.0) * (upper_y - center) + diffuse * (left_x + right_x + lower_y + upper_y - 4.0 * center)

def analyze(state_fields, window, lists, counts, x_anchor):
    members = state_fields.shape[0]
    levels = state_fields.shape[1]
    rows_d = lists.shape[0]
    cols_d = lists.shape[1]
    slots = lists.shape[2]
    flat_lists = lists.reshape(rows_d * cols_d, slots)
    chosen = window[:, flat_lists]
    observed_ensemble = chosen[:members]
    ens_mean = lax.optimization_barrier(jnp.mean(observed_ensemble, axis=0))
    perturb = observed_ensemble - ens_mean
    centre_x = x_anchor + (jnp.arange(rows_d) * DB).astype(state_fields.dtype) + 0.5 * (DB - 1)
    centre_y = (jnp.arange(cols_d) * DB).astype(state_fields.dtype) + 0.5 * (DB - 1)
    centre_x = jnp.broadcast_to(centre_x[:, None], (rows_d, cols_d)).reshape(-1)
    centre_y = jnp.broadcast_to(centre_y[None, :], (rows_d, cols_d)).reshape(-1)
    dist_sq = (chosen[members] - centre_x[:, None]) ** 2 + (chosen[members + 1] - centre_y[:, None]) ** 2
    live = (jnp.arange(slots)[None, :] < counts.reshape(-1)[:, None]).astype(state_fields.dtype)
    weight = chosen[members + 3] * jnp.exp(-dist_sq / (2.0 * LOC * LOC)) * live
    weighted = perturb * weight
    identity = jnp.eye(members, dtype=state_fields.dtype)
    gram = jnp.einsum('knm,jnm->nkj', weighted, perturb, precision=lax.Precision.HIGHEST) + (members - 1.0) * identity
    forcing = jnp.einsum('knm,nm->nk', weighted, chosen[members + 2] - ens_mean, precision=lax.Precision.HIGHEST)
    factor = jnp.linalg.cholesky(gram)
    mean_w = jax.scipy.linalg.cho_solve((factor, True), forcing[..., None])[..., 0]
    inverse_l = jax.scipy.linalg.solve_triangular(factor, jnp.broadcast_to(identity, gram.shape), lower=True)
    transform = jnp.sqrt(members - 1.0) * jnp.swapaxes(inverse_l, 1, 2) + mean_w[:, :, None]
    blocks = state_fields.reshape(members, levels, rows_d, DB, cols_d, DB)
    field_mean = lax.optimization_barrier(jnp.mean(blocks, axis=0))
    anomaly = blocks - field_mean
    trans_grid = transform.reshape(rows_d, cols_d, members, members)
    result = field_mean + jnp.einsum('jlaxcy,acjk->klaxcy', anomaly, trans_grid, precision=lax.Precision.HIGHEST)
    return result.reshape(state_fields.shape)

def reference(state, speed_x, speed_y, diffuse, obs_cell, obs_value, obs_errinv, obs_list, obs_count):
    state_fields = state
    for step_idx in range(STEPS):
        padded = jnp.pad(state_fields, ((0, 0), (0, 0), (1, 1), (0, 0)))
        state_fields = advance(state_fields, padded[:, :, :-2], padded[:, :, 2:], speed_x, speed_y, diffuse)
    predicted_state = state_fields
    tile_of = jnp.arange(NOBS).astype(jnp.int32) // OBS_T
    level = obs_cell // (TILE_CELLS_X * CY)
    local_x = obs_cell // CY % TILE_CELLS_X
    local_y = obs_cell % CY
    global_x = tile_of * TILE_CELLS_X + local_x
    flattened_state = level * (NX * CY) + global_x * CY + local_y
    observed_ensemble = predicted_state.reshape(ENSEMBLE_SIZE, -1)[:, flattened_state]
    rows = jnp.concatenate([observed_ensemble, global_x[None].astype(state.dtype), local_y[None].astype(state.dtype), obs_value[None], obs_errinv[None]], axis=0)
    padded_rows = jnp.pad(rows, ((0, 0), (OBS_T, OBS_T)))

    def one_tile(tile_index):
        window = lax.dynamic_slice_in_dim(padded_rows, tile_index * OBS_T, 3 * OBS_T, 1)
        tile_state_fields = lax.dynamic_slice_in_dim(predicted_state, tile_index * TILE_CELLS_X, TILE_CELLS_X, 2)
        lists = lax.dynamic_slice_in_dim(obs_list, tile_index * (TILE_CELLS_X // DB), TILE_CELLS_X // DB, 0)
        counts = lax.dynamic_slice_in_dim(obs_count, tile_index * (TILE_CELLS_X // DB), TILE_CELLS_X // DB, 0)
        return analyze(tile_state_fields, window, lists, counts, (tile_index * TILE_CELLS_X).astype(state.dtype))
    tiles_out = lax.map(one_tile, jnp.arange(N_TILE).astype(jnp.int32))
    return jnp.moveaxis(tiles_out, 0, 2).reshape(ENSEMBLE_SIZE, LEVELS, NX, CY)
```

```python
import functools

import jax
import jax.numpy as jnp
from jax import lax
from jax.experimental import pallas as pl
from jax.experimental.pallas import tpu as pltpu
from jax.sharding import PartitionSpec as P

STEPS = 4
DB = 2
LOC = 4
LANES = 128
SUB = 8
GROUP = ("section", "mem")
F32 = jnp.float32
BF16 = jnp.bfloat16


def split_2(value):
    high = value.astype(BF16)
    return high, (value - high.astype(F32)).astype(BF16)


def pack_kernel(state_ref, sx_ref, sy_ref, diff_ref, low_ref, high_ref):
    fields, width_x, _ = state_ref.shape
    levels = sx_ref.shape[0]
    for out_ref, start in ((low_ref, 0), (high_ref, width_x - STEPS)):
        rows = pl.ds(start, STEPS)
        for i in range(fields):
            out_ref[pl.ds(i * STEPS, STEPS), :] = state_ref[i, rows, :]
        for i in range(levels):
            out_ref[pl.ds((fields + i) * STEPS, STEPS), :] = sx_ref[i, rows, :]
            out_ref[pl.ds((fields + levels + i) * STEPS, STEPS), :] = sy_ref[i, rows, :]
        out_ref[pl.ds((fields + 2 * levels) * STEPS, STEPS), :] = diff_ref[rows, :]


def pack(state, speed_x, speed_y, diffuse):
    memb_dev, levels, width_x, width_y = state.shape
    fields = memb_dev * levels
    rows = -(-(fields + 2 * levels + 1) * STEPS // SUB) * SUB
    return pl.pallas_call(
        pack_kernel,
        out_shape=[jax.ShapeDtypeStruct((rows, width_y), F32)] * 2,
        name="pack",
    )(state.reshape(fields, width_x, width_y), speed_x, speed_y, diffuse)


def forecast_kernel(
    share, state_ref, low_ref, high_ref, sx_ref, sy_ref, diff_ref, cell_ref, fc_ref, obs_ref, ext_ref, all_ref
):
    fields, width_x, width_y = state_ref.shape
    levels = sx_ref.shape[0]
    memb_dev = fields // levels
    wide = width_x + 2 * STEPS
    inner = pl.ds(STEPS, width_x)

    def widen(slot, own):
        ext_ref[slot, 0:STEPS, :] = low_ref[pl.ds(slot * STEPS, STEPS), :]
        ext_ref[slot, STEPS + width_x : wide, :] = high_ref[pl.ds(slot * STEPS, STEPS), :]
        ext_ref[slot, inner, :] = own

    for i in range(fields):
        widen(i, state_ref[i])
    for i in range(levels):
        widen(fields + i, sx_ref[i])
        widen(fields + levels + i, sy_ref[i])
    widen(fields + 2 * levels, diff_ref[...])

    lane = lax.broadcasted_iota(jnp.int32, (wide, width_y), 1)

    @pl.loop(0, levels)
    def _(level):
        diff = ext_ref[fields + 2 * levels]
        sx = ext_ref[fields + level]
        sy = ext_ref[fields + levels + level]
        from_low = jnp.maximum(sx, 0.0) + diff
        from_high = diff - jnp.minimum(sx, 0.0)
        y_low = jnp.maximum(sy, 0.0) + diff
        y_high = diff - jnp.minimum(sy, 0.0)
        keep = 1.0 - (from_low + from_high + y_low + y_high)
        y_low = jnp.where(lane == 0, 0.0, y_low)
        y_high = jnp.where(lane == width_y - 1, 0.0, y_high)
        for member in range(memb_dev):
            q = ext_ref[member * levels + level]
            for _ in range(STEPS):
                q = (
                    keep * q
                    + from_low * pltpu.roll(q, 1, 0)
                    + from_high * pltpu.roll(q, wide - 1, 0)
                    + y_low * pltpu.roll(q, 1, 1)
                    + y_high * pltpu.roll(q, width_y - 1, 1)
                )
            all_ref[member, pl.ds(level * width_x, width_x), :] = q[STEPS : STEPS + width_x, :]

    for group in range(width_x // share):
        for member in range(memb_dev):
            for row in range(share):
                fc_ref[group, member, pl.ds(row * levels, levels), :] = all_ref[
                    member, pl.ds(group * share + row, levels, stride=width_x), :
                ]

    cell = cell_ref[...]
    obs = cell.shape[1]
    cell_row = cell // width_y
    cell_y = cell - cell_row * width_y
    rows = levels * width_x
    pick = (lax.broadcasted_iota(jnp.int32, (rows, obs), 0) == cell_row).astype(F32).astype(BF16)
    pick_y = lax.broadcasted_iota(jnp.int32, (width_y, obs), 0) == cell_y
    dims = (((0,), (0,)), ((), ()))
    for member in range(memb_dev):
        high, low = split_2(all_ref[member])
        found = lax.dot_general(high, pick, dims, preferred_element_type=F32)
        found = found + lax.dot_general(low, pick, dims, preferred_element_type=F32)
        obs_ref[pl.ds(member, 1), :] = jnp.sum(jnp.where(pick_y, found, 0.0), axis=0, keepdims=True)


def forecast(state, low, high, speed_x, speed_y, diffuse, obs_cell, share):
    memb_dev, levels, width_x, width_y = state.shape
    fields = memb_dev * levels
    groups = width_x // share
    return pl.pallas_call(
        functools.partial(forecast_kernel, share),
        out_shape=[
            jax.ShapeDtypeStruct((groups, memb_dev, share * levels, width_y), F32),
            jax.ShapeDtypeStruct((memb_dev, obs_cell.shape[0]), F32),
        ],
        scratch_shapes=[
            pltpu.VMEM((fields + 2 * levels + 1, width_x + 2 * STEPS, width_y), F32),
            pltpu.VMEM((memb_dev, levels * width_x, width_y), F32),
        ],
        name="forecast",
    )(state.reshape(fields, width_x, width_y), low, high, speed_x, speed_y, diffuse, obs_cell.reshape(1, -1))


def weight_kernel(place_ref, info_ref, list_ref, count_ref, weight_ref):
    domains, slots = list_ref.shape
    obs = info_ref.shape[2]
    limit = float((8 * LOC) ** 2)
    slot = lax.broadcasted_iota(jnp.int32, (domains, slots), 1)
    last = jnp.sum(
        jnp.where(slot == count_ref[...] - 1, list_ref[...], 0).astype(F32), axis=1, keepdims=True
    )
    centre_x = place_ref[0].astype(F32)
    centre_y = lax.broadcasted_iota(jnp.int32, (domains, 1), 0).astype(F32) * (2.0 * DB) + (DB - 1.0)

    def distance(tile):
        delta_x = 2.0 * info_ref[tile, 0:1, :] - centre_x
        delta_y = 2.0 * info_ref[tile, 1:2, :] - centre_y
        return delta_x * delta_x + delta_y * delta_y

    def score_of(tile, dist):
        inside = jnp.minimum(dist, limit)
        if tile == 0:
            inside = jnp.where(place_ref[1] > 0, inside, limit)
        if tile == 2:
            inside = jnp.where(place_ref[2] > 0, inside, limit)
        column = lax.broadcasted_iota(jnp.int32, (1, obs), 1).astype(F32) + float(tile * obs)
        return inside * float(3 * obs) + column, column

    bound = jnp.zeros((domains, 1), F32)
    for tile in range(3):
        score, column = score_of(tile, distance(tile))
        bound = bound + jnp.sum(jnp.where(column == last, score, 0.0), axis=1, keepdims=True)
    for tile in range(3):
        dist = distance(tile)
        score, _ = score_of(tile, dist)
        weight = info_ref[tile, 3:4, :] * jnp.exp(dist * (-1.0 / (8.0 * LOC * LOC)))
        high, low = split_2(jnp.where(score <= bound, weight, 0.0))
        weight_ref[0:domains, pl.ds(tile * obs, obs)] = high
        weight_ref[domains : 2 * domains, pl.ds(tile * obs, obs)] = low


def weights(place, info, lists, counts):
    domains = lists.shape[0]
    vmem = pl.BlockSpec(memory_space=pltpu.VMEM)
    return pl.pallas_call(
        weight_kernel,
        in_specs=[pl.BlockSpec(memory_space=pltpu.SMEM), vmem, vmem, vmem],
        out_specs=vmem,
        out_shape=jax.ShapeDtypeStruct((2 * domains, 3 * info.shape[2]), BF16),
        name="weights",
    )(place, info, lists, counts)


def pair_rows(members):
    half = 2 * SUB
    starts = [half * (k // half) for k in range(members)]
    offsets, total = [], 0
    for start in starts:
        offsets.append(total)
        total += members - start
    return starts, offsets, total


def transform_kernel(ens_ref, info_ref, weight_ref, inv_ref, mean_ref, y_ref, zh_ref, zl_ref, gram_ref, low_ref, s_ref):
    groups, triple, obs = ens_ref.shape
    memb_dev = triple // 3
    members = groups * memb_dev
    starts, offsets, total = pair_rows(members)
    sums = None
    for tile in range(3):
        for group in range(groups):
            y_ref[pl.ds(group * memb_dev, memb_dev), :] = ens_ref[group, pl.ds(tile * memb_dev, memb_dev), :]
        ens = y_ref[...]
        ens_mean = jnp.mean(ens, axis=0, keepdims=True)
        y = ens - ens_mean
        y_ref[...] = y
        for k in range(members):
            prod = y[starts[k] :, :] * y_ref[pl.ds(k, 1), :]
            high, low = split_2(prod)
            zh_ref[pl.ds(offsets[k], members - starts[k]), :] = high
            zl_ref[pl.ds(offsets[k], members - starts[k]), :] = low
        high, low = split_2(y * (info_ref[tile, 2:3, :] - ens_mean))
        zh_ref[pl.ds(total, members), :] = high
        zl_ref[pl.ds(total, members), :] = low
        dims = (((1,), (1,)), ((), ()))
        weight = weight_ref[:, pl.ds(tile * obs, obs)]
        part = lax.dot_general(zh_ref[...], weight, dims, preferred_element_type=F32)
        part = part + lax.dot_general(zl_ref[...], weight, dims, preferred_element_type=F32)
        sums = part if sums is None else sums + part

    width = sums.shape[1]
    domain = lax.broadcasted_iota(jnp.int32, (width, LANES), 0) % (width // 2)
    column = lax.broadcasted_iota(jnp.int32, (width, LANES), 1) // DB
    spread = (domain == column).astype(F32).astype(BF16)
    high, low = split_2(sums)
    rest = (sums - high.astype(F32) - low.astype(F32)).astype(BF16)
    gram = jnp.dot(high, spread, preferred_element_type=F32)
    gram = gram + jnp.dot(low, spread, preferred_element_type=F32)
    gram = gram + jnp.dot(rest, spread, preferred_element_type=F32)
    gram_ref[...] = gram

    sub_row = lax.broadcasted_iota(jnp.int32, (SUB, LANES), 0)

    def every(ref, row):
        return ref[pl.ds(row, SUB, stride=0), :]

    blocks = members // SUB
    mean = [jnp.zeros((SUB, LANES), F32) for _ in range(blocks)]
    for k in range(members):
        own = k // SUB
        acc = [gram_ref[pl.ds(offsets[k] - starts[k] + b * SUB, SUB), :] for b in range(own, blocks)]
        acc[0] = acc[0] + jnp.where(sub_row == k % SUB, members - 1.0, 0.0)
        inv = [jnp.zeros((SUB, LANES), F32) for _ in range(own)]
        inv.append(jnp.where(sub_row == k % SUB, 1.0, 0.0))
        forced = every(gram_ref, total + k)
        for j in range(k):
            base = offsets[j] - starts[j]
            factor = every(low_ref, base + k)
            for b in range(own, blocks):
                acc[b - own] = acc[b - own] - low_ref[pl.ds(base + b * SUB, SUB), :] * factor
            for b in range(j // SUB + 1):
                inv[b] = inv[b] - inv_ref[j, pl.ds(b * SUB, SUB), :] * factor
            forced = forced - s_ref[j] * factor
        pivot = jnp.broadcast_to(acc[0][k % SUB : k % SUB + 1, :], (SUB, LANES))
        scale = lax.rsqrt(pivot)
        scale = scale * (1.5 - 0.5 * pivot * scale * scale)
        for b in range(own, blocks):
            low_ref[pl.ds(offsets[k] - starts[k] + b * SUB, SUB), :] = acc[b - own] * scale
        forced = forced * scale
        s_ref[k] = forced
        for b in range(own + 1):
            inv[b] = inv[b] * scale
            inv_ref[k, pl.ds(b * SUB, SUB), :] = inv[b]
            mean[b] = mean[b] + inv[b] * forced
    for b in range(blocks):
        mean_ref[pl.ds(b * SUB, SUB), :] = mean[b]


def transforms(ens, info, weight):
    groups, triple, obs = ens.shape
    members = groups * triple // 3
    _, _, total = pair_rows(members)
    return pl.pallas_call(
        transform_kernel,
        out_shape=[
            jax.ShapeDtypeStruct((members, members, LANES), F32),
            jax.ShapeDtypeStruct((members, LANES), F32),
        ],
        scratch_shapes=[
            pltpu.VMEM((members, obs), F32),
            pltpu.VMEM((total + members, obs), BF16),
            pltpu.VMEM((total + members, obs), BF16),
            pltpu.VMEM((total + members, LANES), F32),
            pltpu.VMEM((total, LANES), F32),
            pltpu.VMEM((members, SUB, LANES), F32),
        ],
        name="transform",
    )(ens, info, weight)


def apply_kernel(field_ref, inv_ref, mean_ref, out_ref):
    groups, memb_dev, rows, _ = field_ref.shape
    members = groups * memb_dev
    root = float(members - 1) ** 0.5

    @pl.loop(0, rows // SUB)
    def _(block):
        at = pl.ds(pl.multiple_of(block * SUB, SUB), SUB)
        fields = [field_ref[j // memb_dev, j % memb_dev, at, :] for j in range(members)]
        total = fields[0]
        for j in range(1, members):
            total = total + fields[j]
        mean = total * (1.0 / members)
        fields = [field - mean for field in fields]
        base = mean
        for j in range(members):
            base = base + fields[j] * mean_ref[pl.ds(j, SUB, stride=0), :]
        for k in range(members):
            acc = fields[0] * inv_ref[k, pl.ds(0, SUB, stride=0), :]
            for j in range(1, k + 1):
                acc = acc + fields[j] * inv_ref[k, pl.ds(j, SUB, stride=0), :]
            out_ref[k // memb_dev, k % memb_dev, at, :] = base + root * acc


def apply_transform(fields, inverse, mean):
    return pl.pallas_call(
        apply_kernel,
        out_shape=jax.ShapeDtypeStruct(fields.shape, F32),
        name="apply",
    )(fields, inverse, mean)


def unpack_kernel(share, in_ref, out_ref):
    groups, memb_dev, rows, _ = in_ref.shape
    levels = rows // share
    width_x = groups * share
    for group in range(groups):
        for member in range(memb_dev):
            for row in range(share):
                out_ref[member, pl.ds(group * share + row, levels, stride=width_x), :] = in_ref[
                    group, member, pl.ds(row * levels, levels), :
                ]


def unpack(parts, share):
    groups, memb_dev, rows, width_y = parts.shape
    return pl.pallas_call(
        functools.partial(unpack_kernel, share),
        out_shape=jax.ShapeDtypeStruct((memb_dev, groups * rows, width_y), F32),
        name="unpack",
    )(parts)


def neighbours(low, high):
    count = lax.axis_size("tile")
    up = [(i, i + 1) for i in range(count - 1)]
    down = [(i + 1, i) for i in range(count - 1)]
    return lax.ppermute(high, "tile", up), lax.ppermute(low, "tile", down)


def local(state, speed_x, speed_y, diffuse, obs_cell, obs_value, obs_errinv, obs_list, obs_count):
    memb_dev, levels, width_x, width_y = state.shape
    groups = lax.axis_size(GROUP)
    tiles = lax.axis_size("tile")
    tile_index = lax.axis_index("tile")
    group_idx = lax.axis_index(GROUP)
    share = width_x // groups
    obs = obs_cell.shape[0]

    low, high = pack(state, speed_x, speed_y, diffuse)
    low, high = neighbours(low, high)
    fields, own_obs = forecast(state, low, high, speed_x, speed_y, diffuse, obs_cell, share)
    received = lax.all_to_all(fields, GROUP, 0, 0, tiled=True)

    global_x = (tile_index * width_x + obs_cell // width_y % width_x).astype(F32)
    local_y = (obs_cell % width_y).astype(F32)
    rows = jnp.concatenate(
        [own_obs, jnp.stack([global_x, local_y, obs_value, obs_errinv])], axis=0
    )
    below, above = neighbours(rows, rows)
    window = jnp.stack([below, rows, above])
    info = window[:, memb_dev:]
    ens = window[:, :memb_dev].reshape(1, 3 * memb_dev, obs)
    ens = lax.all_to_all(
        jnp.broadcast_to(ens, (groups, 3 * memb_dev, obs)), GROUP, 0, 0, tiled=True
    )

    share_d = share // DB
    lists = lax.dynamic_slice_in_dim(obs_list, group_idx * share_d, share_d, 0).reshape(-1, obs_list.shape[2])
    counts = lax.dynamic_slice_in_dim(obs_count, group_idx * share_d, share_d, 0).reshape(-1, 1)
    place = jnp.stack(
        [
            2 * (tile_index * width_x + group_idx * share) + DB - 1,
            (tile_index > 0).astype(jnp.int32),
            (tile_index < tiles - 1).astype(jnp.int32),
        ]
    )
    weight = weights(place, info, lists, counts)
    inverse, mean = transforms(ens, info, weight)
    analysed = apply_transform(received, inverse, mean)
    back = lax.all_to_all(analysed, GROUP, 0, 0, tiled=True)
    return unpack(back, share).reshape(state.shape)


def solution(mesh):
    placed = (
        P(GROUP, None, "tile", None),
        P(None, "tile", None),
        P(None, "tile", None),
        P("tile", None),
        P("tile"),
        P("tile"),
        P("tile"),
        P("tile", None, None),
        P("tile", None),
    )
    return jax.shard_map(
        local,
        mesh=mesh,
        in_specs=placed,
        out_specs=P(GROUP, None, "tile", None),
        check_vma=False,
    )
```

```python
import functools

import jax
import jax.numpy as jnp
from jax import lax
from jax.experimental import pallas as pl
from jax.experimental.pallas import tpu as pltpu
from jax.sharding import PartitionSpec as P

STEPS = 4
DB = 2
LOC = 4
LANES = 128
SUB = 8
LEVELS_AT_ONCE = 4
GROUP = ("section", "mem")
F32 = jnp.float32
BF16 = jnp.bfloat16
VMEM_LIMIT = 24 * 2**20


CENTRE, PARITY, SECTION, MEM, HAS_A, HAS_B, TILE_X = range(7)


def call(kernel, name, outs, place, *args, scratch=()):
    vmem = pl.BlockSpec(memory_space=pltpu.VMEM)
    outs = [pltpu.VMEM(shape, dtype) for shape, dtype in outs]
    return pl.pallas_call(
        kernel,
        in_specs=[pl.BlockSpec(memory_space=pltpu.SMEM)] + [vmem] * len(args),
        out_specs=[vmem] * len(outs),
        out_shape=outs,
        scratch_shapes=list(scratch),
        compiler_params=pltpu.CompilerParams(vmem_limit_bytes=VMEM_LIMIT),
        name=name,
    )(place, *[pltpu.with_memory_space_constraint(a, pltpu.VMEM) for a in args])


def split_2(value):
    high = value.astype(BF16)
    return high, (value - high.astype(F32)).astype(BF16)


def pack_kernel(
    place_ref, state_ref, sx_ref, sy_ref, diff_ref, cell_ref, value_ref, err_ref, a_ref, b_ref, info_ref
):
    fields, width_x, width_y = state_ref.shape
    levels = sx_ref.shape[0]
    even = place_ref[PARITY] == 0
    base_x = place_ref[TILE_X]

    def put(slot, rows):
        low, high = rows[:STEPS, :], rows[width_x - STEPS :, :]
        at = pl.ds(slot * STEPS, STEPS)
        a_ref[at, :] = jnp.where(even, high, low)
        b_ref[at, :] = jnp.where(even, low, high)

    for i in range(fields):
        put(i, state_ref[i])
    for i in range(levels):
        put(fields + i, sx_ref[i])
        put(fields + levels + i, sy_ref[i])
    put(fields + 2 * levels, diff_ref[...])

    cell = cell_ref[...]
    row = cell // width_y
    rows = cell.shape[0]
    info_ref[0:rows, :] = (base_x + row % width_x).astype(F32)
    info_ref[rows : 2 * rows, :] = (cell - row * width_y).astype(F32)
    info_ref[2 * rows : 3 * rows, :] = value_ref[...]
    info_ref[3 * rows : 4 * rows, :] = err_ref[...]
    start = a_ref.shape[0] - 4 * rows
    a_ref[pl.ds(start, 4 * rows), :] = info_ref[...]
    b_ref[pl.ds(start, 4 * rows), :] = info_ref[...]


def pack(place, state, speed_x, speed_y, diffuse, obs_cell, obs_value, obs_errinv):
    memb_dev, levels, width_x, width_y = state.shape
    fields = memb_dev * levels
    chunks = obs_cell.shape[0] // LANES
    rows = -(-(fields + 2 * levels + 1) * STEPS // SUB) * SUB + 4 * chunks
    return call(
        pack_kernel,
        "pack",
        [((rows, width_y), F32), ((rows, width_y), F32), ((4 * chunks, LANES), F32)],
        place,
        state.reshape(fields, width_x, width_y),
        speed_x,
        speed_y,
        diffuse,
        obs_cell.reshape(chunks, LANES),
        obs_value.reshape(chunks, LANES),
        obs_errinv.reshape(chunks, LANES),
    )


def forecast_kernel(
    share, mems, place_ref, state_ref, a_ref, b_ref, sx_ref, sy_ref, diff_ref, cell_ref, *refs
):
    part_refs, (obs_ref, ext_ref, all_ref) = refs[:mems], refs[mems:]
    fields, width_x, width_y = state_ref.shape
    levels = sx_ref.shape[0]
    memb_dev = fields // levels
    wide = width_x + 2 * STEPS
    even = place_ref[PARITY] == 0

    def widen(slot, own):
        a = a_ref[pl.ds(slot * STEPS, STEPS), :]
        b = b_ref[pl.ds(slot * STEPS, STEPS), :]
        ext_ref[slot, 0:STEPS, :] = jnp.where(even, b, a)
        ext_ref[slot, STEPS : STEPS + width_x, :] = own
        ext_ref[slot, STEPS + width_x : wide, :] = jnp.where(even, a, b)

    for i in range(fields):
        widen(i, state_ref[i])
    for i in range(levels):
        widen(fields + i, sx_ref[i])
        widen(fields + levels + i, sy_ref[i])
    widen(fields + 2 * levels, diff_ref[...])

    lane = lax.broadcasted_iota(jnp.int32, (wide, width_y), 1)
    diff = ext_ref[fields + 2 * levels]
    at_once = LEVELS_AT_ONCE if levels % LEVELS_AT_ONCE == 0 else 1

    @pl.loop(0, levels // at_once)
    def _(block):
        coefs, fields_q = [], []
        for i in range(at_once):
            level = block * at_once + i
            sx = ext_ref[fields + level]
            sy = ext_ref[fields + levels + level]
            from_low = jnp.maximum(sx, 0.0) + diff
            from_high = diff - jnp.minimum(sx, 0.0)
            y_low = jnp.maximum(sy, 0.0) + diff
            y_high = diff - jnp.minimum(sy, 0.0)
            keep = 1.0 - (from_low + from_high + y_low + y_high)
            y_low = jnp.where(lane == 0, 0.0, y_low)
            y_high = jnp.where(lane == width_y - 1, 0.0, y_high)
            coefs.append((keep, from_low, from_high, y_low, y_high))
            fields_q.append([ext_ref[member * levels + level] for member in range(memb_dev)])
        for _ in range(STEPS):
            for i in range(at_once):
                keep, from_low, from_high, y_low, y_high = coefs[i]
                for member in range(memb_dev):
                    q = fields_q[i][member]
                    fields_q[i][member] = (
                        keep * q
                        + from_low * pltpu.roll(q, 1, 0)
                        + from_high * pltpu.roll(q, wide - 1, 0)
                        + y_low * pltpu.roll(q, 1, 1)
                        + y_high * pltpu.roll(q, width_y - 1, 1)
                    )
        for i in range(at_once):
            for member in range(memb_dev):
                all_ref[member, pl.ds((block * at_once + i) * width_x, width_x), :] = fields_q[i][member][
                    STEPS : STEPS + width_x, :
                ]

    for k in range(mems):
        for slot in range(2):
            group = (place_ref[SECTION] ^ slot) * mems + (place_ref[MEM] ^ k)
            for member in range(memb_dev):
                for row in range(share):
                    part_refs[k][slot, member, pl.ds(row * levels, levels), :] = all_ref[
                        member, pl.ds(group * share + row, levels, stride=width_x), :
                    ]

    cell = cell_ref[...]
    obs = cell.shape[1]
    cell_row = cell // width_y
    cell_y = cell - cell_row * width_y
    rows = levels * width_x
    pick = (lax.broadcasted_iota(jnp.int32, (rows, obs), 0) == cell_row).astype(F32).astype(BF16)
    pick_y = lax.broadcasted_iota(jnp.int32, (width_y, obs), 0) == cell_y
    dims = (((0,), (0,)), ((), ()))
    for member in range(memb_dev):
        high, low = split_2(all_ref[member])
        found = lax.dot_general(high, pick, dims, preferred_element_type=F32)
        found = found + lax.dot_general(low, pick, dims, preferred_element_type=F32)
        obs_ref[pl.ds(member, 1), :] = jnp.sum(jnp.where(pick_y, found, 0.0), axis=0, keepdims=True)


def forecast(place, state, a, b, speed_x, speed_y, diffuse, obs_cell, share, mems):
    memb_dev, levels, width_x, width_y = state.shape
    fields = memb_dev * levels
    out = call(
        functools.partial(forecast_kernel, share, mems),
        "forecast",
        [((2, memb_dev, share * levels, width_y), F32)] * mems + [((memb_dev, obs_cell.shape[0]), F32)],
        place,
        state.reshape(fields, width_x, width_y),
        a,
        b,
        speed_x,
        speed_y,
        diffuse,
        obs_cell.reshape(1, -1),
        scratch=[
            pltpu.VMEM((fields + 2 * levels + 1, width_x + 2 * STEPS, width_y), F32),
            pltpu.VMEM((memb_dev, levels * width_x, width_y), F32),
        ],
    )
    return out[:mems], out[mems]


def info_row(ref, start, chunk):
    return ref[pl.ds(start + chunk, 1), :]


def weight_kernel(place_ref, list_ref, count_ref, own_ref, a_ref, b_ref, weight_ref):
    domains, slots = list_ref.shape
    chunks = own_ref.shape[0] // 4
    obs = chunks * LANES
    limit = float((8 * LOC) ** 2)
    slot = lax.broadcasted_iota(jnp.int32, (domains, slots), 1)
    last = jnp.sum(
        jnp.where(slot == count_ref[...] - 1, list_ref[...], 0).astype(F32), axis=1, keepdims=True
    )
    centre_x = place_ref[CENTRE].astype(F32)
    centre_y = lax.broadcasted_iota(jnp.int32, (domains, 1), 0).astype(F32) * (2.0 * DB) + (DB - 1.0)
    parity = place_ref[PARITY]
    tail = a_ref.shape[0] - 4 * chunks
    sources = (
        (own_ref, 0, 1, None),
        (a_ref, tail, 2 - 2 * parity, place_ref[HAS_A]),
        (b_ref, tail, 2 * parity, place_ref[HAS_B]),
    )

    def chunk_of(source, chunk):
        ref, start, tile_slot, present = source
        delta_x = 2.0 * info_row(ref, start, chunk) - centre_x
        delta_y = 2.0 * info_row(ref, start + chunks, chunk) - centre_y
        dist = delta_x * delta_x + delta_y * delta_y
        inside = jnp.minimum(dist, limit)
        if present is not None:
            inside = jnp.where(present > 0, inside, limit)
        first = jnp.asarray(tile_slot * obs + chunk * LANES, jnp.int32)
        column = (lax.broadcasted_iota(jnp.int32, (1, LANES), 1) + first).astype(F32)
        return dist, inside * float(3 * obs) + column, column

    found = jnp.zeros((domains, LANES), F32)
    for source in sources:
        for chunk in range(chunks):
            _, score, column = chunk_of(source, chunk)
            found = found + jnp.where(column == last, score, 0.0)
    bound = jnp.sum(found, axis=1, keepdims=True)
    for n, source in enumerate(sources):
        ref, start, _, _ = source
        for chunk in range(chunks):
            dist, score, _ = chunk_of(source, chunk)
            weight = info_row(ref, start + 3 * chunks, chunk) * jnp.exp(dist * (-1.0 / (8.0 * LOC * LOC)))
            high, low = split_2(jnp.where(score <= bound, weight, 0.0))
            at = pl.ds(n * obs + chunk * LANES, LANES)
            weight_ref[0:domains, at] = high
            weight_ref[domains : 2 * domains, at] = low


def weights(place, lists, counts, own, a, b):
    domains = lists.shape[0]
    columns = 3 * (own.shape[0] // 4) * LANES
    return call(
        weight_kernel, "weights", [((2 * domains, columns), BF16)], place, lists, counts, own, a, b
    )[0]


def pair_rows(members):
    half = 2 * SUB
    starts = [half * (k // half) for k in range(members)]
    offsets, total = [], 0
    for start in starts:
        offsets.append(total)
        total += members - start
    return starts, offsets, total


def gram_of(place_ref, mems, ens_refs, info_ref, info_start, weight, y_ref, zh_ref, zl_ref):
    obs = y_ref.shape[1]
    chunks = obs // LANES
    members = y_ref.shape[0]
    memb_dev = members // (2 * mems)
    starts, offsets, total = pair_rows(members)
    for section in range(2):
        here = place_ref[SECTION] == section
        for mem in range(mems):
            k = place_ref[MEM] ^ mem
            rows = jnp.where(here, ens_refs[0][k], ens_refs[1][k])
            y_ref[pl.ds((section * mems + mem) * memb_dev, memb_dev), :] = rows
    ens = y_ref[...]
    ens_mean = jnp.mean(ens, axis=0, keepdims=True)
    y = ens - ens_mean
    y_ref[...] = y
    for k in range(members):
        high, low = split_2(y[starts[k] :, :] * y_ref[pl.ds(k, 1), :])
        zh_ref[pl.ds(offsets[k], members - starts[k]), :] = high
        zl_ref[pl.ds(offsets[k], members - starts[k]), :] = low
    value = jnp.concatenate([info_row(info_ref, info_start + 2 * chunks, c) for c in range(chunks)], axis=1)
    high, low = split_2(y * (value - ens_mean))
    zh_ref[pl.ds(total, members), :] = high
    zl_ref[pl.ds(total, members), :] = low
    dims = (((1,), (1,)), ((), ()))
    part = lax.dot_general(zh_ref[...], weight, dims, preferred_element_type=F32)
    return part + lax.dot_general(zl_ref[...], weight, dims, preferred_element_type=F32)


def gram_scratch(members, obs):
    _, _, total = pair_rows(members)
    return [
        pltpu.VMEM((members, obs), F32),
        pltpu.VMEM((total + members, obs), BF16),
        pltpu.VMEM((total + members, obs), BF16),
    ]


def own_gram_kernel(mems, place_ref, own_ref, partner_ref, info_ref, weight_ref, out_ref, y_ref, zh_ref, zl_ref):
    obs = y_ref.shape[1]
    out_ref[...] = gram_of(
        place_ref, mems, (own_ref, partner_ref), info_ref, 0, weight_ref[:, 0:obs], y_ref, zh_ref, zl_ref
    )


def own_gram(place, own, partner, info, weight, mems):
    members, obs = 2 * mems * own.shape[1], own.shape[2]
    _, _, total = pair_rows(members)
    return call(
        functools.partial(own_gram_kernel, mems),
        "own_gram",
        [((total + members, weight.shape[0]), F32)],
        place,
        own,
        partner,
        info,
        weight,
        scratch=gram_scratch(members, obs),
    )[0]


def transform_kernel(
    mems,
    place_ref,
    part_ref,
    za_ref,
    zb_ref,
    zp_ref,
    a_ref,
    b_ref,
    weight_ref,
    inv_ref,
    mean_ref,
    y_ref,
    zh_ref,
    zl_ref,
    gram_ref,
    low_ref,
    s_ref,
):
    obs = y_ref.shape[1]
    members = y_ref.shape[0]
    starts, offsets, total = pair_rows(members)
    sums = part_ref[...]
    start = a_ref.shape[0] - 4 * obs // LANES
    for n, (near_ref, info_ref) in enumerate(((za_ref, a_ref), (zb_ref, b_ref))):
        sums = sums + gram_of(
            place_ref,
            mems,
            (near_ref, zp_ref.at[n]),
            info_ref,
            start,
            weight_ref[:, pl.ds((n + 1) * obs, obs)],
            y_ref,
            zh_ref,
            zl_ref,
        )

    width = sums.shape[1]
    domain = lax.broadcasted_iota(jnp.int32, (width, LANES), 0) % (width // 2)
    column = lax.broadcasted_iota(jnp.int32, (width, LANES), 1) // DB
    spread = (domain == column).astype(F32).astype(BF16)
    high, low = split_2(sums)
    rest = (sums - high.astype(F32) - low.astype(F32)).astype(BF16)
    gram = jnp.dot(high, spread, preferred_element_type=F32)
    gram = gram + jnp.dot(low, spread, preferred_element_type=F32)
    gram = gram + jnp.dot(rest, spread, preferred_element_type=F32)
    gram_ref[...] = gram

    sub_row = lax.broadcasted_iota(jnp.int32, (SUB, LANES), 0)

    def every(ref, row):
        return ref[pl.ds(row, SUB, stride=0), :]

    blocks = members // SUB
    inv_ref[...] = jnp.zeros(inv_ref.shape, F32)
    mean = [jnp.zeros((SUB, LANES), F32) for _ in range(blocks)]
    for k in range(members):
        own = k // SUB
        acc = [gram_ref[pl.ds(offsets[k] - starts[k] + b * SUB, SUB), :] for b in range(own, blocks)]
        acc[0] = acc[0] + jnp.where(sub_row == k % SUB, members - 1.0, 0.0)
        inv = [jnp.zeros((SUB, LANES), F32) for _ in range(own)]
        inv.append(jnp.where(sub_row == k % SUB, 1.0, 0.0))
        forced = every(gram_ref, total + k)
        for j in range(k):
            base = offsets[j] - starts[j]
            factor = every(low_ref, base + k)
            for b in range(own, blocks):
                acc[b - own] = acc[b - own] - low_ref[pl.ds(base + b * SUB, SUB), :] * factor
            for b in range(j // SUB + 1):
                inv[b] = inv[b] - inv_ref[j, pl.ds(b * SUB, SUB), :] * factor
            forced = forced - s_ref[j] * factor
        pivot = jnp.broadcast_to(acc[0][k % SUB : k % SUB + 1, :], (SUB, LANES))
        scale = lax.rsqrt(pivot)
        scale = scale * (1.5 - 0.5 * pivot * scale * scale)
        for b in range(own, blocks):
            low_ref[pl.ds(offsets[k] - starts[k] + b * SUB, SUB), :] = acc[b - own] * scale
        forced = forced * scale
        s_ref[k] = forced
        for b in range(own + 1):
            inv[b] = inv[b] * scale
            inv_ref[k, pl.ds(b * SUB, SUB), :] = inv[b]
            mean[b] = mean[b] + inv[b] * forced
    for b in range(blocks):
        mean_ref[pl.ds(b * SUB, SUB), :] = mean[b]


def transforms(place, part, near_a, near_b, partner, a, b, weight, mems):
    members, obs = 2 * mems * near_a.shape[1], near_a.shape[2]
    _, _, total = pair_rows(members)
    return call(
        functools.partial(transform_kernel, mems),
        "transform",
        [((members, members, LANES), F32), ((members, LANES), F32)],
        place,
        part,
        near_a,
        near_b,
        partner,
        a,
        b,
        weight,
        scratch=gram_scratch(members, obs)
        + [
            pltpu.VMEM((total + members, LANES), F32),
            pltpu.VMEM((total, LANES), F32),
            pltpu.VMEM((members, SUB, LANES), F32),
        ],
    )


def centre_kernel(mems, place_ref, *refs):
    near_refs, (far_ref, mean_ref, anomaly_ref, base_ref) = refs[:mems], refs[mems:]
    memb_dev, rows, _ = anomaly_ref.shape[0] // (2 * mems), anomaly_ref.shape[1], None
    members = 2 * mems * memb_dev
    for block in range(rows // SUB):
        at = pl.ds(block * SUB, SUB)
        total = None
        for k in range(mems):
            for i in range(memb_dev):
                pair = near_refs[k][0, i, at, :] + far_ref[k, i, at, :]
                total = pair if total is None else total + pair
        mean = total * (1.0 / members)
        base = mean
        for other in range(2):
            for k in range(mems):
                group = (place_ref[SECTION] ^ other) * mems + (place_ref[MEM] ^ k)
                for i in range(memb_dev):
                    field = far_ref[k, i, at, :] if other else near_refs[k][0, i, at, :]
                    field = field - mean
                    anomaly_ref[group * memb_dev + i, at, :] = field
                    base = base + field * mean_ref[pl.ds(group * memb_dev + i, SUB, stride=0), :]
        base_ref[at, :] = base


def centre(place, near, far, mean, mems):
    _, memb_dev, rows, width_y = near[0].shape
    return call(
        functools.partial(centre_kernel, mems),
        "centre",
        [((2 * mems * memb_dev, rows, width_y), F32), ((rows, width_y), F32)],
        place,
        *near,
        far,
        mean,
    )


def apply_kernel(mems, k, place_ref, anomaly_ref, base_ref, inv_ref, out_ref):
    members, rows, _ = anomaly_ref.shape
    memb_dev = members // (2 * mems)
    root = float(members - 1) ** 0.5
    blocks = rows // SUB
    for slot in range(2):
        group = (place_ref[SECTION] ^ slot) * mems + (place_ref[MEM] ^ k)
        first = group * memb_dev
        zero = tuple(jnp.zeros((SUB, LANES), F32) for _ in range(memb_dev * blocks))

        def step(chunk, acc, first=first):
            acc = list(acc)
            for t in range(memb_dev):
                j = chunk * memb_dev + t
                fields = [anomaly_ref[j, pl.ds(b * SUB, SUB), :] for b in range(blocks)]
                for i in range(memb_dev):
                    factor = inv_ref[first + i, pl.ds(j, SUB, stride=0), :]
                    for b in range(blocks):
                        acc[i * blocks + b] = acc[i * blocks + b] + fields[b] * factor
            return tuple(acc)

        acc = lax.fori_loop(0, group + 1, step, zero)
        for i in range(memb_dev):
            for b in range(blocks):
                at = pl.ds(b * SUB, SUB)
                out_ref[slot, i, at, :] = base_ref[at, :] + root * acc[i * blocks + b]


def apply_transform(place, anomaly, base, inverse, mems, k):
    members, rows, width_y = anomaly.shape
    return call(
        functools.partial(apply_kernel, mems, k),
        "apply",
        [((2, members // (2 * mems), rows, width_y), F32)],
        place,
        anomaly,
        base,
        inverse,
    )[0]


def unpack_kernel(share, mems, place_ref, *refs):
    near_refs, (far_ref, out_ref) = refs[:mems], refs[mems:]
    _, memb_dev, rows, _ = far_ref.shape
    levels = rows // share
    width_x = out_ref.shape[1] // levels
    for other in range(2):
        for k in range(mems):
            group = (place_ref[SECTION] ^ other) * mems + (place_ref[MEM] ^ k)
            for i in range(memb_dev):
                for row in range(share):
                    at = pl.ds(row * levels, levels)
                    out_ref[i, pl.ds(group * share + row, levels, stride=width_x), :] = (
                        far_ref[k, i, at, :] if other else near_refs[k][0, i, at, :]
                    )


def unpack(place, near, far, share, mems):
    _, memb_dev, rows, width_y = near[0].shape
    vmem = pl.BlockSpec(memory_space=pltpu.VMEM)
    return pl.pallas_call(
        functools.partial(unpack_kernel, share, mems),
        in_specs=[pl.BlockSpec(memory_space=pltpu.SMEM)] + [vmem] * (mems + 1),
        out_specs=vmem,
        out_shape=jax.ShapeDtypeStruct((memb_dev, 2 * mems * rows, width_y), F32),
        compiler_params=pltpu.CompilerParams(vmem_limit_bytes=VMEM_LIMIT),
        name="unpack",
    )(place, *[pltpu.with_memory_space_constraint(x, pltpu.VMEM) for x in (*near, far)])


def along_tile(first, second):
    count = lax.axis_size("tile")

    def trade(value, start):
        pairs = []
        for i in range(start, count - 1, 2):
            pairs += [(i, i + 1), (i + 1, i)]
        return lax.ppermute(value, "tile", pairs)

    return trade(first, 0), trade(second, 1)


def to_partner(value):
    return lax.ppermute(value, "section", [(0, 1), (1, 0)])


def over_mem(value, k):
    return lax.ppermute(value, "mem", [(i, i ^ k) for i in range(lax.axis_size("mem"))])


def local(state, speed_x, speed_y, diffuse, obs_cell, obs_value, obs_errinv, obs_list, obs_count):
    memb_dev, levels, width_x, width_y = state.shape
    mems = lax.axis_size("mem")
    groups = lax.axis_size(GROUP)
    assert groups == 2 * mems and mems & (mems - 1) == 0
    tiles = lax.axis_size("tile")
    tile = lax.axis_index("tile")
    group_idx = lax.axis_index(GROUP)
    share = width_x // groups
    far = list(range(mems - 1, 0, -1))

    parity = tile % 2
    place = jnp.stack(
        [
            2 * (tile * width_x + group_idx * share) + DB - 1,
            parity,
            lax.axis_index("section"),
            lax.axis_index("mem"),
            ((parity == 1) | (tile < tiles - 1)).astype(jnp.int32),
            jnp.where(parity == 1, tile < tiles - 1, tile > 0).astype(jnp.int32),
            tile * width_x,
        ]
    ).astype(jnp.int32)

    share_d = share // DB
    lists = lax.dynamic_slice_in_dim(obs_list, group_idx * share_d, share_d, 0).reshape(-1, obs_list.shape[2])
    counts = lax.dynamic_slice_in_dim(obs_count, group_idx * share_d, share_d, 0).reshape(-1, 1)

    a, b, info = pack(place, state, speed_x, speed_y, diffuse, obs_cell, obs_value, obs_errinv)
    a, b = along_tile(a, b)
    parts, own_obs = forecast(place, state, a, b, speed_x, speed_y, diffuse, obs_cell, share, mems)

    gathered = [own_obs] + [over_mem(own_obs, k) for k in range(1, mems)]
    gathered = jnp.stack(gathered)
    near = [parts[0]] + [over_mem(parts[k], k) for k in range(1, mems)]
    near_a, near_b = along_tile(gathered, gathered)
    partner_obs = to_partner(gathered)
    weight = weights(place, lists, counts, info, a, b)
    part = own_gram(place, gathered, partner_obs, info, weight, mems)
    partner_near = to_partner(jnp.stack([near_a, near_b]))
    away = to_partner(jnp.stack([x[1] for x in near]))
    inverse, mean = transforms(place, part, near_a, near_b, partner_near, a, b, weight, mems)
    anomaly, base = centre(place, near, away, mean, mems)

    done = [None] * mems
    for k in far + [0]:
        result = apply_transform(place, anomaly, base, inverse, mems, k)
        done[k] = over_mem(result, k) if k else result
    away = to_partner(jnp.stack([x[1] for x in done]))
    return unpack(place, done, away, share, mems).reshape(state.shape)


def solution(mesh):
    placed = (
        P(GROUP, None, "tile", None),
        P(None, "tile", None),
        P(None, "tile", None),
        P("tile", None),
        P("tile"),
        P("tile"),
        P("tile"),
        P("tile", None, None),
        P("tile", None),
    )
    return jax.shard_map(
        local,
        mesh=mesh,
        in_specs=placed,
        out_specs=P(GROUP, None, "tile", None),
        check_vma=False,
    )
```

```python
import functools

import jax
import jax.numpy as jnp
from jax import lax
from jax.experimental import pallas as pl
from jax.experimental.pallas import tpu as pltpu
from jax.sharding import PartitionSpec as P

STEPS = 4
DB = 2
LOC = 4
LANES = 128
SUB = 8
LEVELS_AT_ONCE = 4
GROUP = ("section", "mem")
F32 = jnp.float32
BF16 = jnp.bfloat16
VMEM_LIMIT = 24 * 2**20


CENTRE, PARITY, SECTION, MEM, HAS_A, HAS_B, TILE_X = range(7)


def call(kernel, outs, place, *args, scratch=(), inputs=pltpu.VMEM):
    vmem = pl.BlockSpec(memory_space=pltpu.VMEM)
    outs = [pltpu.VMEM(shape, dtype) for shape, dtype in outs]
    return pl.pallas_call(
        kernel,
        in_specs=[pl.BlockSpec(memory_space=pltpu.SMEM)] + [vmem] * len(args),
        out_specs=[vmem] * len(outs),
        out_shape=outs,
        scratch_shapes=list(scratch),
        compiler_params=pltpu.CompilerParams(vmem_limit_bytes=VMEM_LIMIT),
    )(place, *[pltpu.with_memory_space_constraint(a, inputs) for a in args])


def split_2(value):
    high = value.astype(BF16)
    return high, (value - high.astype(F32)).astype(BF16)


def pack_kernel(
    place_ref, state_ref, sx_ref, sy_ref, diff_ref, cell_ref, value_ref, err_ref, a_ref, b_ref, info_ref
):
    fields, width_x, width_y = state_ref.shape
    levels = sx_ref.shape[0]
    even = place_ref[PARITY] == 0
    cell = cell_ref[...]
    row = cell // width_y
    rows = cell.shape[0]
    info_ref[0:rows, :] = (place_ref[TILE_X] + row % width_x).astype(F32)
    info_ref[rows : 2 * rows, :] = (cell - row * width_y).astype(F32)
    info_ref[2 * rows : 3 * rows, :] = value_ref[...]
    info_ref[3 * rows : 4 * rows, :] = err_ref[...]
    at = lax.broadcasted_iota(jnp.int32, (STEPS, width_y), 0)

    def put(slot, values):
        low, high = values[:STEPS, :], values[width_x - STEPS :, :]
        extra = slot - fields
        if 0 <= extra < 4 * rows:
            line = info_ref[extra : extra + 1, :]
            low = jnp.where(at == STEPS - 1, line, low)
            high = jnp.where(at == 0, line, high)
        a_ref[slot] = jnp.where(even, high, low)
        b_ref[slot] = jnp.where(even, low, high)

    for i in range(fields):
        put(i, state_ref[i])
    for i in range(levels):
        put(fields + i, sx_ref[i])
        put(fields + levels + i, sy_ref[i])
    put(fields + 2 * levels, diff_ref[...])


def pack(place, state, speed_x, speed_y, diffuse, obs_cell, obs_value, obs_errinv):
    memb_dev, levels, width_x, width_y = state.shape
    fields = memb_dev * levels
    chunks = obs_cell.shape[0] // LANES
    slots = fields + 2 * levels + 1
    assert 4 * chunks <= 2 * levels + 1 and width_y == LANES
    return call(
        pack_kernel,
        [((slots, STEPS, width_y), F32), ((slots, STEPS, width_y), F32), ((4 * chunks, LANES), F32)],
        place,
        state.reshape(fields, width_x, width_y),
        speed_x,
        speed_y,
        diffuse,
        obs_cell.reshape(chunks, LANES),
        obs_value.reshape(chunks, LANES),
        obs_errinv.reshape(chunks, LANES),
        inputs=pltpu.HBM,
    )


def forecast_kernel(
    share,
    mems,
    place_ref,
    state_ref,
    a_ref,
    b_ref,
    sx_ref,
    sy_ref,
    diff_ref,
    cell_ref,
    keep_ref,
    send_ref,
    obs_ref,
    all_ref,
):
    fields, width_x, width_y = state_ref.shape
    levels = sx_ref.shape[0]
    memb_dev = fields // levels
    wide = width_x + 2 * STEPS
    even = place_ref[PARITY] == 0

    def ring(slot, own):
        first, second = a_ref[slot], b_ref[slot]
        above, below = jnp.where(even, first, second), jnp.where(even, second, first)
        return jnp.concatenate([own, above, below], axis=0)

    lane = lax.broadcasted_iota(jnp.int32, (wide, width_y), 1)
    diff = ring(fields + 2 * levels, diff_ref[...])
    at_once = LEVELS_AT_ONCE if levels % LEVELS_AT_ONCE == 0 else 1

    @pl.loop(0, levels // at_once)
    def _(block):
        coefs, fields_q = [], []
        for i in range(at_once):
            level = block * at_once + i
            sx = ring(fields + level, sx_ref[level])
            sy = ring(fields + levels + level, sy_ref[level])
            from_low = jnp.maximum(sx, 0.0) + diff
            from_high = diff - jnp.minimum(sx, 0.0)
            y_low = jnp.maximum(sy, 0.0) + diff
            y_high = diff - jnp.minimum(sy, 0.0)
            keep = 1.0 - (from_low + from_high + y_low + y_high)
            y_low = jnp.where(lane == 0, 0.0, y_low)
            y_high = jnp.where(lane == width_y - 1, 0.0, y_high)
            coefs.append((keep, from_low, from_high, y_low, y_high))
            fields_q.append(
                [ring(m * levels + level, state_ref[m * levels + level]) for m in range(memb_dev)]
            )
        for _ in range(STEPS):
            for i in range(at_once):
                keep, from_low, from_high, y_low, y_high = coefs[i]
                for member in range(memb_dev):
                    q = fields_q[i][member]
                    fields_q[i][member] = (
                        keep * q
                        + from_low * pltpu.roll(q, 1, 0)
                        + from_high * pltpu.roll(q, wide - 1, 0)
                        + y_low * pltpu.roll(q, 1, 1)
                        + y_high * pltpu.roll(q, width_y - 1, 1)
                    )
        for i in range(at_once):
            for member in range(memb_dev):
                at = pl.ds(pl.multiple_of((block * at_once + i) * width_x, SUB), width_x)
                all_ref[member, at, :] = fields_q[i][member][:width_x, :]

    for k in range(mems):
        for slot, part_ref in enumerate((keep_ref, send_ref)):
            group = (place_ref[SECTION] ^ slot) * mems + (place_ref[MEM] ^ k)
            for member in range(memb_dev):
                for row in range(share):
                    part_ref[k, member, pl.ds(row * levels, levels), :] = all_ref[
                        member, pl.ds(group * share + row, levels, stride=width_x), :
                    ]

    cell = cell_ref[...]
    obs = cell.shape[1]
    cell_row = cell // width_y
    cell_y = cell - cell_row * width_y
    rows = levels * width_x
    pick = (lax.broadcasted_iota(jnp.int32, (rows, obs), 0) == cell_row).astype(F32).astype(BF16)
    pick_y = lax.broadcasted_iota(jnp.int32, (width_y, obs), 0) == cell_y
    dims = (((0,), (0,)), ((), ()))
    for member in range(memb_dev):
        high, low = split_2(all_ref[member])
        found = lax.dot_general(high, pick, dims, preferred_element_type=F32)
        found = found + lax.dot_general(low, pick, dims, preferred_element_type=F32)
        obs_ref[pl.ds(member, 1), :] = jnp.sum(jnp.where(pick_y, found, 0.0), axis=0, keepdims=True)


def forecast(place, state, a, b, speed_x, speed_y, diffuse, obs_cell, share, mems):
    memb_dev, levels, width_x, width_y = state.shape
    fields = memb_dev * levels
    return call(
        functools.partial(forecast_kernel, share, mems),
        [((mems, memb_dev, share * levels, width_y), F32)] * 2 + [((memb_dev, obs_cell.shape[0]), F32)],
        place,
        state.reshape(fields, width_x, width_y),
        a,
        b,
        speed_x,
        speed_y,
        diffuse,
        obs_cell.reshape(1, -1),
        scratch=[
            pltpu.VMEM((memb_dev, levels * width_x, width_y), F32),
        ],
    )


def join_kernel(place_ref, keep_ref, other_ref, *out_refs):
    for k, out_ref in enumerate(out_refs):
        out_ref[0] = keep_ref[k + 1]
        out_ref[1] = other_ref[k + 1]


def join(place, keep, other):
    mems, *rest = keep.shape
    return call(join_kernel, [((2, *rest), F32)] * (mems - 1), place, keep, other)


def info_reader(place_ref, ref, fields, first):
    if fields is None:
        return lambda row: ref[row : row + 1, :]
    above = (place_ref[PARITY] == 0) == first

    def read(row):
        return jnp.where(above, ref[fields + row, STEPS - 1 :, :], ref[fields + row, 0:1, :])

    return read


def weight_kernel(fields, place_ref, list_ref, count_ref, own_ref, a_ref, b_ref, weight_ref):
    domains, slots = list_ref.shape
    chunks = own_ref.shape[0] // 4
    obs = chunks * LANES
    limit = float((8 * LOC) ** 2)
    slot = lax.broadcasted_iota(jnp.int32, (domains, slots), 1)
    last = jnp.sum(
        jnp.where(slot == count_ref[...] - 1, list_ref[...], 0).astype(F32), axis=1, keepdims=True
    )
    centre_x = place_ref[CENTRE].astype(F32)
    centre_y = lax.broadcasted_iota(jnp.int32, (domains, 1), 0).astype(F32) * (2.0 * DB) + (DB - 1.0)
    parity = place_ref[PARITY]
    sources = (
        (info_reader(place_ref, own_ref, None, None), 1, None),
        (info_reader(place_ref, a_ref, fields, True), 2 - 2 * parity, place_ref[HAS_A]),
        (info_reader(place_ref, b_ref, fields, False), 2 * parity, place_ref[HAS_B]),
    )

    def chunk_of(source, chunk):
        read, tile_slot, present = source
        delta_x = 2.0 * read(chunk) - centre_x
        delta_y = 2.0 * read(chunks + chunk) - centre_y
        dist = delta_x * delta_x + delta_y * delta_y
        inside = jnp.minimum(dist, limit)
        if present is not None:
            inside = jnp.where(present > 0, inside, limit)
        first = jnp.asarray(tile_slot * obs + chunk * LANES, jnp.int32)
        column = (lax.broadcasted_iota(jnp.int32, (1, LANES), 1) + first).astype(F32)
        return dist, inside * float(3 * obs) + column, column

    found = jnp.zeros((domains, LANES), F32)
    for source in sources:
        for chunk in range(chunks):
            _, score, column = chunk_of(source, chunk)
            found = found + jnp.where(column == last, score, 0.0)
    bound = jnp.sum(found, axis=1, keepdims=True)
    for n, source in enumerate(sources):
        for chunk in range(chunks):
            dist, score, _ = chunk_of(source, chunk)
            weight = source[0](3 * chunks + chunk) * jnp.exp(dist * (-1.0 / (8.0 * LOC * LOC)))
            high, low = split_2(jnp.where(score <= bound, weight, 0.0))
            at = pl.ds(n * obs + chunk * LANES, LANES)
            weight_ref[0:domains, at] = high
            weight_ref[domains : 2 * domains, at] = low


def weights(place, lists, counts, own, a, b, fields):
    domains = lists.shape[0]
    columns = 3 * (own.shape[0] // 4) * LANES
    kernel = functools.partial(weight_kernel, fields)
    return call(kernel, [((2 * domains, columns), BF16)], place, lists, counts, own, a, b)[0]


def pair_rows(members):
    starts = [SUB * (k // SUB) for k in range(members)]
    offsets, total = [], 0
    for start in starts:
        offsets.append(total)
        total += members - start
    return starts, offsets, total


def gram_of(place_ref, ens_ref, read, weight, y_ref, zh_ref, zl_ref):
    members, obs = y_ref.shape
    chunks = obs // LANES
    mems, _, memb_dev, _ = ens_ref.shape
    starts, offsets, total = pair_rows(members)
    for section in range(2):
        for mem in range(mems):
            rows = ens_ref[place_ref[MEM] ^ mem, place_ref[SECTION] ^ section]
            y_ref[pl.ds((section * mems + mem) * memb_dev, memb_dev), :] = rows
    ens = y_ref[...]
    ens_mean = jnp.mean(ens, axis=0, keepdims=True)
    y = ens - ens_mean
    y_ref[...] = y
    for k in range(0, members, 2):
        tail = y[starts[k] :, :]
        both = jnp.concatenate([tail * y_ref[k : k + 1, :], tail * y_ref[k + 1 : k + 2, :]], axis=0)
        high, low = split_2(both)
        zh_ref[pl.ds(offsets[k], both.shape[0]), :] = high
        zl_ref[pl.ds(offsets[k], both.shape[0]), :] = low
    value = jnp.concatenate([read(2 * chunks + c) for c in range(chunks)], axis=1)
    high, low = split_2(y * (value - ens_mean))
    zh_ref[pl.ds(total, members), :] = high
    zl_ref[pl.ds(total, members), :] = low
    dims = (((1,), (1,)), ((), ()))
    part = lax.dot_general(zh_ref[...], weight, dims, preferred_element_type=F32)
    return part + lax.dot_general(zl_ref[...], weight, dims, preferred_element_type=F32)


def gram_scratch(members, obs):
    _, _, total = pair_rows(members)
    return [
        pltpu.VMEM((members, obs), F32),
        pltpu.VMEM((total + members, obs), BF16),
        pltpu.VMEM((total + members, obs), BF16),
    ]


def own_gram_kernel(place_ref, own_ref, info_ref, weight_ref, out_ref, y_ref, zh_ref, zl_ref):
    read = info_reader(place_ref, info_ref, None, None)
    weight = weight_ref[:, 0 : y_ref.shape[1]]
    out_ref[...] = gram_of(place_ref, own_ref, read, weight, y_ref, zh_ref, zl_ref)


def ensemble(gathered):
    mems, sections, memb_dev, obs = gathered.shape
    return mems * sections * memb_dev, obs


def own_gram(place, own, info, weight):
    members, obs = ensemble(own)
    _, _, total = pair_rows(members)
    return call(
        own_gram_kernel,
        [((total + members, weight.shape[0]), F32)],
        place,
        own,
        info,
        weight,
        scratch=gram_scratch(members, obs),
    )[0]


def anomalies(place_ref, keep_ref, other_ref, near_refs, anomaly_ref, base_ref):
    members, rows, _ = anomaly_ref.shape
    mems = len(near_refs) + 1
    memb_dev = members // (2 * mems)

    def field_of(other, k, i, at):
        if k:
            return near_refs[k - 1][other, i, at, :]
        return other_ref[0, i, at, :] if other else keep_ref[0, i, at, :]

    for block in range(rows // SUB):
        at = pl.ds(block * SUB, SUB)
        fields = [
            (other, k, i, field_of(other, k, i, at))
            for other in range(2)
            for k in range(mems)
            for i in range(memb_dev)
        ]
        mean = sum(field for *_, field in fields) * (1.0 / members)
        base_ref[at, :] = mean
        for other, k, i, field in fields:
            member = ((place_ref[SECTION] ^ other) * mems + (place_ref[MEM] ^ k)) * memb_dev + i
            anomaly_ref[member, at, :] = field - mean


def transform_kernel(mems, fields, place_ref, part_ref, za_ref, zb_ref, a_ref, b_ref, weight_ref, *refs):
    keep_ref, other_ref, near_refs, refs = refs[0], refs[1], refs[2 : mems + 1], refs[mems + 1 :]
    inv_ref, anomaly_ref, base_ref, y_ref, zh_ref, zl_ref, gram_ref, low_ref, s_ref = refs
    obs = y_ref.shape[1]
    members = y_ref.shape[0]
    starts, offsets, total = pair_rows(members)
    sums = part_ref[...]
    for n, (near_ref, info_ref) in enumerate(((za_ref, a_ref), (zb_ref, b_ref))):
        read = info_reader(place_ref, info_ref, fields, n == 0)
        weight = weight_ref[:, pl.ds((n + 1) * obs, obs)]
        sums = sums + gram_of(place_ref, near_ref, read, weight, y_ref, zh_ref, zl_ref)
    anomalies(place_ref, keep_ref, other_ref, near_refs, anomaly_ref, base_ref)

    width = sums.shape[1]
    domain = lax.broadcasted_iota(jnp.int32, (width, LANES), 0) % (width // 2)
    column = lax.broadcasted_iota(jnp.int32, (width, LANES), 1) // DB
    spread = (domain == column).astype(F32).astype(BF16)
    high, low = split_2(sums)
    rest = (sums - high.astype(F32) - low.astype(F32)).astype(BF16)
    gram = jnp.dot(high, spread, preferred_element_type=F32)
    gram = gram + jnp.dot(low, spread, preferred_element_type=F32)
    gram = gram + jnp.dot(rest, spread, preferred_element_type=F32)
    gram_ref[...] = gram

    sub_row = lax.broadcasted_iota(jnp.int32, (SUB, LANES), 0)

    def every(ref, row):
        return ref[pl.ds(row, SUB, stride=0), :]

    blocks = members // SUB
    inv_ref[...] = jnp.zeros(inv_ref.shape, F32)
    mean = [jnp.zeros((SUB, LANES), F32) for _ in range(blocks)]
    for k in range(members):
        own = k // SUB
        acc = [gram_ref[pl.ds(offsets[k] - starts[k] + b * SUB, SUB), :] for b in range(own, blocks)]
        acc[0] = acc[0] + jnp.where(sub_row == k % SUB, members - 1.0, 0.0)
        inv = [jnp.zeros((SUB, LANES), F32) for _ in range(own)]
        inv.append(jnp.where(sub_row == k % SUB, 1.0, 0.0))
        forced = every(gram_ref, total + k)
        for j in range(k):
            base = offsets[j] - starts[j]
            factor = every(low_ref, base + k)
            for b in range(own, blocks):
                acc[b - own] = acc[b - own] - low_ref[pl.ds(base + b * SUB, SUB), :] * factor
            for b in range(j // SUB + 1):
                inv[b] = inv[b] - inv_ref[j, pl.ds(b * SUB, SUB), :] * factor
            forced = forced - s_ref[j] * factor
        pivot = jnp.broadcast_to(acc[0][k % SUB : k % SUB + 1, :], (SUB, LANES))
        scale = lax.rsqrt(pivot)
        scale = scale * (1.5 - 0.5 * pivot * scale * scale)
        for b in range(own, blocks):
            low_ref[pl.ds(offsets[k] - starts[k] + b * SUB, SUB), :] = acc[b - own] * scale
        forced = forced * scale
        s_ref[k] = forced
        for b in range(own + 1):
            inv[b] = inv[b] * scale
            inv_ref[k, pl.ds(b * SUB, SUB), :] = inv[b]
            mean[b] = mean[b] + inv[b] * forced
    for row in range(base_ref.shape[0] // SUB):
        at = pl.ds(row * SUB, SUB)
        base = base_ref[at, :]
        for j in range(members):
            shift = jnp.broadcast_to(mean[j // SUB][j % SUB : j % SUB + 1, :], (SUB, LANES))
            base = base + anomaly_ref[j, at, :] * shift
        base_ref[at, :] = base


def transforms(place, part, near_a, near_b, a, b, weight, keep, other, near, fields):
    members, obs = ensemble(near_a)
    _, _, total = pair_rows(members)
    rows = keep.shape[2]
    return call(
        functools.partial(transform_kernel, keep.shape[0], fields),
        [
            ((members, members, LANES), F32),
            ((members, rows, LANES), F32),
            ((rows, LANES), F32),
        ],
        place,
        part,
        near_a,
        near_b,
        a,
        b,
        weight,
        keep,
        other,
        *near,
        scratch=gram_scratch(members, obs)
        + [
            pltpu.VMEM((total + members, LANES), F32),
            pltpu.VMEM((total, LANES), F32),
            pltpu.VMEM((members, SUB, LANES), F32),
        ],
    )


def apply_kernel(mems, k, place_ref, anomaly_ref, base_ref, inv_ref, *out_refs):
    members, rows, _ = anomaly_ref.shape
    memb_dev = members // (2 * mems)
    root = float(members - 1) ** 0.5
    blocks = rows // SUB
    if len(out_refs) == 1:
        out_refs = [out_refs[0].at[slot] for slot in range(2)]
    for slot in range(2):
        group = (place_ref[SECTION] ^ slot) * mems + (place_ref[MEM] ^ k)
        first = group * memb_dev
        zero = tuple(jnp.zeros((SUB, LANES), F32) for _ in range(memb_dev * blocks))

        def step(chunk, acc, first=first):
            acc = list(acc)
            for t in range(memb_dev):
                j = chunk * memb_dev + t
                fields = [anomaly_ref[j, pl.ds(b * SUB, SUB), :] for b in range(blocks)]
                for i in range(memb_dev):
                    factor = inv_ref[first + i, pl.ds(j, SUB, stride=0), :]
                    for b in range(blocks):
                        acc[i * blocks + b] = acc[i * blocks + b] + fields[b] * factor
            return tuple(acc)

        acc = lax.fori_loop(0, group + 1, step, zero)
        for i in range(memb_dev):
            for b in range(blocks):
                at = pl.ds(b * SUB, SUB)
                out_refs[slot][i, at, :] = base_ref[at, :] + root * acc[i * blocks + b]


def apply_transform(place, anomaly, base, inverse, mems, k, split):
    members, rows, width_y = anomaly.shape
    block = (members // (2 * mems), rows, width_y)
    outs = [(block, F32)] * 2 if split else [((2, *block), F32)]
    return call(functools.partial(apply_kernel, mems, k), outs, place, anomaly, base, inverse)


def unpack_kernel(share, mems, place_ref, *refs):
    near_refs, far_refs, (out_ref, all_ref, sem_ref) = refs[:mems], refs[mems : 2 * mems], refs[2 * mems :]
    memb_dev, total, _ = all_ref.shape
    levels = total // (2 * mems * share)
    width_x = total // levels
    copies = []
    for i in range(memb_dev):
        for other in range(2):
            for k in range(mems):
                group = (place_ref[SECTION] ^ other) * mems + (place_ref[MEM] ^ k)
                block_ref = (far_refs if other else near_refs)[k]
                if len(block_ref.shape) == 4:
                    block_ref = block_ref.at[other]
                for row in range(share):
                    all_ref[i, pl.ds(group * share + row, levels, stride=width_x), :] = block_ref[
                        i, pl.ds(row * levels, levels), :
                    ]
        copies.append(pltpu.make_async_copy(all_ref.at[i], out_ref.at[i], sem_ref.at[i]))
        copies[-1].start()
    for copy in copies:
        copy.wait()


def unpack(place, near, far, share, mems):
    memb_dev, rows, width_y = near[0].shape[-3:]
    vmem = pl.BlockSpec(memory_space=pltpu.VMEM)
    shape = (memb_dev, 2 * mems * rows, width_y)
    return pl.pallas_call(
        functools.partial(unpack_kernel, share, mems),
        in_specs=[pl.BlockSpec(memory_space=pltpu.SMEM)] + [vmem] * (2 * mems),
        out_specs=pl.BlockSpec(memory_space=pltpu.HBM),
        out_shape=jax.ShapeDtypeStruct(shape, F32),
        scratch_shapes=[pltpu.VMEM(shape, F32), pltpu.SemaphoreType.DMA((memb_dev,))],
        compiler_params=pltpu.CompilerParams(vmem_limit_bytes=VMEM_LIMIT),
        name="unpack",
    )(place, *[pltpu.with_memory_space_constraint(x, pltpu.VMEM) for x in (*near, *far)])


def along_tile(first, second):
    count = lax.axis_size("tile")

    def trade(value, start):
        pairs = []
        for i in range(start, count - 1, 2):
            pairs += [(i, i + 1), (i + 1, i)]
        return lax.ppermute(value, "tile", pairs)

    first = trade(first, 0)
    second = trade(second, 1)
    return first, second


def to_partner(value):
    return lax.ppermute(value, "section", [(0, 1), (1, 0)])


def over_mem(value, k):
    return lax.ppermute(value, "mem", [(i, i ^ k) for i in range(lax.axis_size("mem"))])


def across(value, k):
    size = lax.axis_size(GROUP)
    return lax.ppermute(value, GROUP, [(i, i ^ (size // 2) ^ k) for i in range(size)])


def analysis(state, speed_x, speed_y, diffuse, obs_cell, obs_value, obs_errinv, obs_list, obs_count):
    memb_dev, levels, width_x, _ = state.shape
    mems = lax.axis_size("mem")
    groups = lax.axis_size(GROUP)
    assert groups == 2 * mems and mems & (mems - 1) == 0
    tiles = lax.axis_size("tile")
    tile = lax.axis_index("tile")
    group_idx = lax.axis_index(GROUP)
    share = width_x // groups
    far = list(range(mems - 1, 0, -1))

    parity = tile % 2
    place = jnp.stack(
        [
            2 * (tile * width_x + group_idx * share) + DB - 1,
            parity,
            lax.axis_index("section"),
            lax.axis_index("mem"),
            ((parity == 1) | (tile < tiles - 1)).astype(jnp.int32),
            jnp.where(parity == 1, tile < tiles - 1, tile > 0).astype(jnp.int32),
            tile * width_x,
        ]
    ).astype(jnp.int32)

    share_d = share // DB
    lists = lax.dynamic_slice_in_dim(obs_list, group_idx * share_d, share_d, 0)
    lists = lists.reshape(-1, obs_list.shape[2])
    counts = lax.dynamic_slice_in_dim(obs_count, group_idx * share_d, share_d, 0).reshape(-1, 1)

    a, b, info = pack(place, state, speed_x, speed_y, diffuse, obs_cell, obs_value, obs_errinv)
    a, b = along_tile(a, b)
    keep, send, own_obs = forecast(
        place, state, a, b, speed_x, speed_y, diffuse, obs_cell, share, mems
    )

    other_obs = to_partner(own_obs)
    other = to_partner(send)
    both_obs = jnp.stack([own_obs, other_obs])
    gathered = [both_obs] + [over_mem(both_obs, k) for k in far[::-1]]
    gathered = jnp.stack(gathered)
    joined = join(place, keep, other)
    near = [over_mem(joined[k - 1], k) for k in far[::-1]]
    near_a, near_b = along_tile(gathered, gathered)
    weight = weights(place, lists, counts, info, a, b, memb_dev * levels)
    part = own_gram(place, gathered, info, weight)
    inverse, anomaly, base = transforms(
        place, part, near_a, near_b, a, b, weight, keep, other, near, memb_dev * levels
    )

    direct = None
    done, away = [None] * mems, [None] * mems
    for k in far + [0]:
        result = apply_transform(place, anomaly, base, inverse, mems, k, k == direct)
        done[k] = over_mem(result[0], k) if k else result[0]
        if k == direct:
            away[k] = across(result[1], k)
    for k in range(mems):
        if k != direct:
            away[k] = to_partner(done[k])
    return unpack(place, done, away, share, mems).reshape(state.shape)


def solution(mesh):
    placed = (
        P(GROUP, None, "tile", None),
        P(None, "tile", None),
        P(None, "tile", None),
        P("tile", None),
        P("tile"),
        P("tile"),
        P("tile"),
        P("tile", None, None),
        P("tile", None),
    )
    return jax.shard_map(
        analysis,
        mesh=mesh,
        in_specs=placed,
        out_specs=P(GROUP, None, "tile", None),
        check_vma=False,
    )
```

```python
import functools

import jax
import jax.numpy as jnp
from jax import lax
from jax.experimental import pallas as pl
from jax.experimental.pallas import tpu as pltpu
from jax.sharding import PartitionSpec as P

STEPS = 4
DB = 2
LOC = 4
LANES = 128
SUB = 8
LEVELS_AT_ONCE = 4
GROUP = ("section", "mem")
F32 = jnp.float32
BF16 = jnp.bfloat16
VMEM_LIMIT = 24 * 2**20


CENTRE, PARITY, SECTION, MEM, HAS_A, HAS_B, TILE_X = range(7)


def position(tiles, width_x, share, mems):
    tile, section, mem = (lax.axis_index(name) for name in ("tile", "section", "mem"))
    parity = tile % 2
    above, below = (tile < tiles - 1).astype(jnp.int32), (tile > 0).astype(jnp.int32)
    first = 2 * (tile * width_x + (section * mems + mem) * share) + DB - 1
    has_a = jnp.where(parity == 1, below, above)
    has_b = jnp.where(parity == 1, above, below)
    return first, parity, section, mem, has_a, has_b, tile * width_x


def call(kernel, outs, place, *args, scratch=(), inputs=pltpu.VMEM):
    vmem = pl.BlockSpec(memory_space=pltpu.VMEM)
    outs = [pltpu.VMEM(shape, dtype) for shape, dtype in outs]
    return pl.pallas_call(
        lambda *refs: kernel(position(*place), *refs),
        in_specs=[vmem] * len(args),
        out_specs=[vmem] * len(outs),
        out_shape=outs,
        scratch_shapes=list(scratch),
        compiler_params=pltpu.CompilerParams(vmem_limit_bytes=VMEM_LIMIT),
    )(*[pltpu.with_memory_space_constraint(a, inputs) for a in args])


def split_2(value):
    high = value.astype(BF16)
    return high, (value - high.astype(F32)).astype(BF16)


def pack_kernel(
    place_ref, state_ref, sx_ref, sy_ref, diff_ref, cell_ref, value_ref, err_ref, a_ref, b_ref, info_ref
):
    fields, width_x, width_y = state_ref.shape
    levels = sx_ref.shape[0]
    even = place_ref[PARITY] == 0
    cell = cell_ref[...]
    row = cell // width_y
    rows = cell.shape[0]
    info_ref[0:rows, :] = (place_ref[TILE_X] + row % width_x).astype(F32)
    info_ref[rows : 2 * rows, :] = (cell - row * width_y).astype(F32)
    info_ref[2 * rows : 3 * rows, :] = value_ref[...]
    info_ref[3 * rows : 4 * rows, :] = err_ref[...]
    at = lax.broadcasted_iota(jnp.int32, (STEPS, width_y), 0)

    def put(slot, values):
        low, high = values[:STEPS, :], values[width_x - STEPS :, :]
        extra = slot - fields
        if 0 <= extra < 4 * rows:
            line = info_ref[extra : extra + 1, :]
            low = jnp.where(at == STEPS - 1, line, low)
            high = jnp.where(at == 0, line, high)
        a_ref[slot] = jnp.where(even, high, low)
        b_ref[slot] = jnp.where(even, low, high)

    for i in range(fields):
        put(i, state_ref[i])
    for i in range(levels):
        put(fields + i, sx_ref[i])
        put(fields + levels + i, sy_ref[i])
    put(fields + 2 * levels, diff_ref[...])


def pack(place, state, speed_x, speed_y, diffuse, obs_cell, obs_value, obs_errinv):
    memb_dev, levels, width_x, width_y = state.shape
    fields = memb_dev * levels
    chunks = obs_cell.shape[0] // LANES
    slots = fields + 2 * levels + 1
    assert 4 * chunks <= 2 * levels + 1 and width_y == LANES
    return call(
        pack_kernel,
        [((slots, STEPS, width_y), F32), ((slots, STEPS, width_y), F32), ((4 * chunks, LANES), F32)],
        place,
        state.reshape(fields, width_x, width_y),
        speed_x,
        speed_y,
        diffuse,
        obs_cell.reshape(chunks, LANES),
        obs_value.reshape(chunks, LANES),
        obs_errinv.reshape(chunks, LANES),
        inputs=pltpu.HBM,
    )


def forecast_kernel(
    share,
    mems,
    place_ref,
    state_ref,
    a_ref,
    b_ref,
    sx_ref,
    sy_ref,
    diff_ref,
    cell_ref,
    keep_ref,
    send_ref,
    obs_ref,
    all_ref,
):
    fields, width_x, width_y = state_ref.shape
    levels = sx_ref.shape[0]
    memb_dev = fields // levels
    wide = width_x + 2 * STEPS
    even = place_ref[PARITY] == 0

    def ring(slot, own):
        first, second = a_ref[slot], b_ref[slot]
        above, below = jnp.where(even, first, second), jnp.where(even, second, first)
        return jnp.concatenate([own, above, below], axis=0)

    lane = lax.broadcasted_iota(jnp.int32, (wide, width_y), 1)
    diff = ring(fields + 2 * levels, diff_ref[...])
    at_once = LEVELS_AT_ONCE if levels % LEVELS_AT_ONCE == 0 else 1

    @pl.loop(0, levels // at_once)
    def _(block):
        coefs, fields_q = [], []
        for i in range(at_once):
            level = block * at_once + i
            sx = ring(fields + level, sx_ref[level])
            sy = ring(fields + levels + level, sy_ref[level])
            from_low = jnp.maximum(sx, 0.0) + diff
            from_high = diff - jnp.minimum(sx, 0.0)
            y_low = jnp.maximum(sy, 0.0) + diff
            y_high = diff - jnp.minimum(sy, 0.0)
            keep = 1.0 - (from_low + from_high + y_low + y_high)
            y_low = jnp.where(lane == 0, 0.0, y_low)
            y_high = jnp.where(lane == width_y - 1, 0.0, y_high)
            coefs.append((keep, from_low, from_high, y_low, y_high))
            fields_q.append(
                [ring(m * levels + level, state_ref[m * levels + level]) for m in range(memb_dev)]
            )
        for _ in range(STEPS):
            for i in range(at_once):
                keep, from_low, from_high, y_low, y_high = coefs[i]
                for member in range(memb_dev):
                    q = fields_q[i][member]
                    fields_q[i][member] = (
                        keep * q
                        + from_low * pltpu.roll(q, 1, 0)
                        + from_high * pltpu.roll(q, wide - 1, 0)
                        + y_low * pltpu.roll(q, 1, 1)
                        + y_high * pltpu.roll(q, width_y - 1, 1)
                    )
        for i in range(at_once):
            for member in range(memb_dev):
                at = pl.ds(pl.multiple_of((block * at_once + i) * width_x, SUB), width_x)
                all_ref[member, at, :] = fields_q[i][member][:width_x, :]

    for k in range(mems):
        for slot, part_ref in enumerate((keep_ref, send_ref)):
            group = (place_ref[SECTION] ^ slot) * mems + (place_ref[MEM] ^ k)
            for member in range(memb_dev):
                for row in range(share):
                    part_ref[k, member, pl.ds(row * levels, levels), :] = all_ref[
                        member, pl.ds(group * share + row, levels, stride=width_x), :
                    ]

    cell = cell_ref[...]
    obs = cell.shape[1]
    cell_row = cell // width_y
    cell_y = cell - cell_row * width_y
    rows = levels * width_x
    pick = (lax.broadcasted_iota(jnp.int32, (rows, obs), 0) == cell_row).astype(F32).astype(BF16)
    pick_y = lax.broadcasted_iota(jnp.int32, (width_y, obs), 0) == cell_y
    dims = (((0,), (0,)), ((), ()))
    for member in range(memb_dev):
        high, low = split_2(all_ref[member])
        found = lax.dot_general(high, pick, dims, preferred_element_type=F32)
        found = found + lax.dot_general(low, pick, dims, preferred_element_type=F32)
        obs_ref[pl.ds(member, 1), :] = jnp.sum(jnp.where(pick_y, found, 0.0), axis=0, keepdims=True)


def forecast(place, state, a, b, speed_x, speed_y, diffuse, obs_cell, share, mems):
    memb_dev, levels, width_x, width_y = state.shape
    fields = memb_dev * levels
    return call(
        functools.partial(forecast_kernel, share, mems),
        [((mems, memb_dev, share * levels, width_y), F32)] * 2 + [((memb_dev, obs_cell.shape[0]), F32)],
        place,
        state.reshape(fields, width_x, width_y),
        a,
        b,
        speed_x,
        speed_y,
        diffuse,
        obs_cell.reshape(1, -1),
        scratch=[
            pltpu.VMEM((memb_dev, levels * width_x, width_y), F32),
        ],
    )


def join_kernel(place_ref, keep_ref, other_ref, *out_refs):
    for k, out_ref in enumerate(out_refs):
        out_ref[0] = keep_ref[k + 1]
        out_ref[1] = other_ref[k + 1]


def join(place, keep, other):
    mems, *rest = keep.shape
    return call(join_kernel, [((2, *rest), F32)] * (mems - 1), place, keep, other)


def info_reader(place_ref, ref, fields, first):
    if fields is None:
        return lambda row: ref[row : row + 1, :]
    above = (place_ref[PARITY] == 0) == first

    def read(row):
        return jnp.where(above, ref[fields + row, STEPS - 1 :, :], ref[fields + row, 0:1, :])

    return read


def weight_kernel(fields, place_ref, list_ref, count_ref, own_ref, a_ref, b_ref, weight_ref):
    domains, slots = list_ref.shape
    chunks = own_ref.shape[0] // 4
    obs = chunks * LANES
    limit = float((8 * LOC) ** 2)
    slot = lax.broadcasted_iota(jnp.int32, (domains, slots), 1)
    last = jnp.sum(
        jnp.where(slot == count_ref[...] - 1, list_ref[...], 0).astype(F32), axis=1, keepdims=True
    )
    centre_x = place_ref[CENTRE].astype(F32)
    centre_y = lax.broadcasted_iota(jnp.int32, (domains, 1), 0).astype(F32) * (2.0 * DB) + (DB - 1.0)
    parity = place_ref[PARITY]
    sources = (
        (info_reader(place_ref, own_ref, None, None), 1, None),
        (info_reader(place_ref, a_ref, fields, True), 2 - 2 * parity, place_ref[HAS_A]),
        (info_reader(place_ref, b_ref, fields, False), 2 * parity, place_ref[HAS_B]),
    )

    def chunk_of(source, chunk):
        read, tile_slot, present = source
        delta_x = 2.0 * read(chunk) - centre_x
        delta_y = 2.0 * read(chunks + chunk) - centre_y
        dist = delta_x * delta_x + delta_y * delta_y
        inside = jnp.minimum(dist, limit)
        if present is not None:
            inside = jnp.where(present > 0, inside, limit)
        first = jnp.asarray(tile_slot * obs + chunk * LANES, jnp.int32)
        column = (lax.broadcasted_iota(jnp.int32, (1, LANES), 1) + first).astype(F32)
        return dist, inside * float(3 * obs) + column, column

    found = jnp.zeros((domains, LANES), F32)
    for source in sources:
        for chunk in range(chunks):
            _, score, column = chunk_of(source, chunk)
            found = found + jnp.where(column == last, score, 0.0)
    bound = jnp.sum(found, axis=1, keepdims=True)
    for n, source in enumerate(sources):
        for chunk in range(chunks):
            dist, score, _ = chunk_of(source, chunk)
            weight = source[0](3 * chunks + chunk) * jnp.exp(dist * (-1.0 / (8.0 * LOC * LOC)))
            high, low = split_2(jnp.where(score <= bound, weight, 0.0))
            at = pl.ds(n * obs + chunk * LANES, LANES)
            weight_ref[0:domains, at] = high
            weight_ref[domains : 2 * domains, at] = low


def weights(place, lists, counts, own, a, b, fields):
    domains = lists.shape[0]
    columns = 3 * (own.shape[0] // 4) * LANES
    kernel = functools.partial(weight_kernel, fields)
    return call(kernel, [((2 * domains, columns), BF16)], place, lists, counts, own, a, b)[0]


def pair_rows(members):
    starts = [SUB * (k // SUB) for k in range(members)]
    offsets, total = [], 0
    for start in starts:
        offsets.append(total)
        total += members - start
    return starts, offsets, total


def gram_of(place_ref, ens_ref, read, weight, y_ref, zh_ref, zl_ref):
    members, obs = y_ref.shape
    chunks = obs // LANES
    mems, _, memb_dev, _ = ens_ref.shape
    starts, offsets, total = pair_rows(members)
    for section in range(2):
        for mem in range(mems):
            rows = ens_ref[place_ref[MEM] ^ mem, place_ref[SECTION] ^ section]
            y_ref[pl.ds((section * mems + mem) * memb_dev, memb_dev), :] = rows
    ens = y_ref[...]
    ens_mean = jnp.mean(ens, axis=0, keepdims=True)
    y = ens - ens_mean
    y_ref[...] = y
    for k in range(0, members, 2):
        tail = y[starts[k] :, :]
        both = jnp.concatenate([tail * y_ref[k : k + 1, :], tail * y_ref[k + 1 : k + 2, :]], axis=0)
        high, low = split_2(both)
        zh_ref[pl.ds(offsets[k], both.shape[0]), :] = high
        zl_ref[pl.ds(offsets[k], both.shape[0]), :] = low
    value = jnp.concatenate([read(2 * chunks + c) for c in range(chunks)], axis=1)
    high, low = split_2(y * (value - ens_mean))
    zh_ref[pl.ds(total, members), :] = high
    zl_ref[pl.ds(total, members), :] = low
    dims = (((1,), (1,)), ((), ()))
    part = lax.dot_general(zh_ref[...], weight, dims, preferred_element_type=F32)
    return part + lax.dot_general(zl_ref[...], weight, dims, preferred_element_type=F32)


def gram_scratch(members, obs):
    _, _, total = pair_rows(members)
    return [
        pltpu.VMEM((members, obs), F32),
        pltpu.VMEM((total + members, obs), BF16),
        pltpu.VMEM((total + members, obs), BF16),
    ]


def own_gram_kernel(place_ref, own_ref, info_ref, weight_ref, out_ref, y_ref, zh_ref, zl_ref):
    read = info_reader(place_ref, info_ref, None, None)
    weight = weight_ref[:, 0 : y_ref.shape[1]]
    out_ref[...] = gram_of(place_ref, own_ref, read, weight, y_ref, zh_ref, zl_ref)


def ensemble(gathered):
    mems, sections, memb_dev, obs = gathered.shape
    return mems * sections * memb_dev, obs


def own_gram(place, own, info, weight):
    members, obs = ensemble(own)
    _, _, total = pair_rows(members)
    return call(
        own_gram_kernel,
        [((total + members, weight.shape[0]), F32)],
        place,
        own,
        info,
        weight,
        scratch=gram_scratch(members, obs),
    )[0]


def centre_kernel(place_ref, keep_ref, other_ref, *refs):
    near_refs, (mean_ref, anomaly_ref, base_ref) = refs[:-3], refs[-3:]
    members, rows, _ = anomaly_ref.shape
    mems = len(near_refs) + 1
    memb_dev = members // (2 * mems)

    def field_of(other, k, i, at):
        if k:
            return near_refs[k - 1][other, i, at, :]
        return other_ref[0, i, at, :] if other else keep_ref[0, i, at, :]

    for block in range(rows // SUB):
        at = pl.ds(block * SUB, SUB)
        fields = [
            (other, k, i, field_of(other, k, i, at))
            for other in range(2)
            for k in range(mems)
            for i in range(memb_dev)
        ]
        mean = sum(field for *_, field in fields) * (1.0 / members)
        base = mean
        for other, k, i, field in fields:
            member = ((place_ref[SECTION] ^ other) * mems + (place_ref[MEM] ^ k)) * memb_dev + i
            field = field - mean
            anomaly_ref[member, at, :] = field
            base = base + field * mean_ref[pl.ds(member, SUB, stride=0), :]
        base_ref[at, :] = base


def centre(place, keep, other, near, mean):
    mems, memb_dev, rows, width_y = keep.shape
    outs = [((2 * mems * memb_dev, rows, width_y), F32), ((rows, width_y), F32)]
    return call(centre_kernel, outs, place, keep, other, *near, mean)


def transform_kernel(fields, place_ref, part_ref, za_ref, zb_ref, a_ref, b_ref, weight_ref, *refs):
    inv_ref, mean_ref, y_ref, zh_ref, zl_ref, gram_ref, low_ref, s_ref = refs
    obs = y_ref.shape[1]
    members = y_ref.shape[0]
    starts, offsets, total = pair_rows(members)
    sums = part_ref[...]
    for n, (near_ref, info_ref) in enumerate(((za_ref, a_ref), (zb_ref, b_ref))):
        read = info_reader(place_ref, info_ref, fields, n == 0)
        weight = weight_ref[:, pl.ds((n + 1) * obs, obs)]
        sums = sums + gram_of(place_ref, near_ref, read, weight, y_ref, zh_ref, zl_ref)

    width = sums.shape[1]
    domain = lax.broadcasted_iota(jnp.int32, (width, LANES), 0) % (width // 2)
    column = lax.broadcasted_iota(jnp.int32, (width, LANES), 1) // DB
    spread = (domain == column).astype(F32).astype(BF16)
    high, low = split_2(sums)
    rest = (sums - high.astype(F32) - low.astype(F32)).astype(BF16)
    gram = jnp.dot(high, spread, preferred_element_type=F32)
    gram = gram + jnp.dot(low, spread, preferred_element_type=F32)
    gram = gram + jnp.dot(rest, spread, preferred_element_type=F32)
    gram_ref[...] = gram

    sub_row = lax.broadcasted_iota(jnp.int32, (SUB, LANES), 0)

    def every(ref, row):
        return ref[pl.ds(row, SUB, stride=0), :]

    blocks = members // SUB
    inv_ref[...] = jnp.zeros(inv_ref.shape, F32)
    mean = [jnp.zeros((SUB, LANES), F32) for _ in range(blocks)]
    for k in range(members):
        own = k // SUB
        acc = [gram_ref[pl.ds(offsets[k] - starts[k] + b * SUB, SUB), :] for b in range(own, blocks)]
        acc[0] = acc[0] + jnp.where(sub_row == k % SUB, members - 1.0, 0.0)
        inv = [jnp.zeros((SUB, LANES), F32) for _ in range(own)]
        inv.append(jnp.where(sub_row == k % SUB, 1.0, 0.0))
        forced = every(gram_ref, total + k)
        for j in range(k):
            base = offsets[j] - starts[j]
            factor = every(low_ref, base + k)
            for b in range(own, blocks):
                acc[b - own] = acc[b - own] - low_ref[pl.ds(base + b * SUB, SUB), :] * factor
            for b in range(j // SUB + 1):
                inv[b] = inv[b] - inv_ref[j, pl.ds(b * SUB, SUB), :] * factor
            forced = forced - s_ref[j] * factor
        pivot = jnp.broadcast_to(acc[0][k % SUB : k % SUB + 1, :], (SUB, LANES))
        scale = lax.rsqrt(pivot)
        scale = scale * (1.5 - 0.5 * pivot * scale * scale)
        for b in range(own, blocks):
            low_ref[pl.ds(offsets[k] - starts[k] + b * SUB, SUB), :] = acc[b - own] * scale
        forced = forced * scale
        s_ref[k] = forced
        for b in range(own + 1):
            inv[b] = inv[b] * scale
            inv_ref[k, pl.ds(b * SUB, SUB), :] = inv[b]
            mean[b] = mean[b] + inv[b] * forced
    for b in range(blocks):
        mean_ref[pl.ds(b * SUB, SUB), :] = mean[b]


def transforms(place, part, near_a, near_b, a, b, weight, fields):
    members, obs = ensemble(near_a)
    _, _, total = pair_rows(members)
    return call(
        functools.partial(transform_kernel, fields),
        [((members, members, LANES), F32), ((members, LANES), F32)],
        place,
        part,
        near_a,
        near_b,
        a,
        b,
        weight,
        scratch=gram_scratch(members, obs)
        + [
            pltpu.VMEM((total + members, LANES), F32),
            pltpu.VMEM((total, LANES), F32),
            pltpu.VMEM((members, SUB, LANES), F32),
        ],
    )


def apply_kernel(mems, k, place_ref, anomaly_ref, base_ref, inv_ref, *out_refs):
    members, rows, _ = anomaly_ref.shape
    memb_dev = members // (2 * mems)
    root = float(members - 1) ** 0.5
    blocks = rows // SUB
    if len(out_refs) == 1:
        out_refs = [out_refs[0].at[slot] for slot in range(2)]
    for slot in range(2):
        group = (place_ref[SECTION] ^ slot) * mems + (place_ref[MEM] ^ k)
        first = group * memb_dev
        zero = tuple(jnp.zeros((SUB, LANES), F32) for _ in range(memb_dev * blocks))

        def step(chunk, acc, first=first):
            acc = list(acc)
            for t in range(memb_dev):
                j = chunk * memb_dev + t
                fields = [anomaly_ref[j, pl.ds(b * SUB, SUB), :] for b in range(blocks)]
                for i in range(memb_dev):
                    factor = inv_ref[first + i, pl.ds(j, SUB, stride=0), :]
                    for b in range(blocks):
                        acc[i * blocks + b] = acc[i * blocks + b] + fields[b] * factor
            return tuple(acc)

        acc = lax.fori_loop(0, group + 1, step, zero)
        for i in range(memb_dev):
            for b in range(blocks):
                at = pl.ds(b * SUB, SUB)
                out_refs[slot][i, at, :] = base_ref[at, :] + root * acc[i * blocks + b]


def apply_transform(place, anomaly, base, inverse, mems, k, split):
    members, rows, width_y = anomaly.shape
    block = (members // (2 * mems), rows, width_y)
    outs = [(block, F32)] * 2 if split else [((2, *block), F32)]
    return call(functools.partial(apply_kernel, mems, k), outs, place, anomaly, base, inverse)


def unpack_kernel(share, mems, place_ref, *refs):
    near_refs, far_refs, (out_ref, all_ref, sem_ref) = refs[:mems], refs[mems : 2 * mems], refs[2 * mems :]
    memb_dev, total, _ = all_ref.shape
    levels = total // (2 * mems * share)
    width_x = total // levels
    copies = []
    for i in range(memb_dev):
        for other in range(2):
            for k in range(mems):
                group = (place_ref[SECTION] ^ other) * mems + (place_ref[MEM] ^ k)
                block_ref = (far_refs if other else near_refs)[k]
                if len(block_ref.shape) == 4:
                    block_ref = block_ref.at[other]
                for row in range(share):
                    all_ref[i, pl.ds(group * share + row, levels, stride=width_x), :] = block_ref[
                        i, pl.ds(row * levels, levels), :
                    ]
        copies.append(pltpu.make_async_copy(all_ref.at[i], out_ref.at[i], sem_ref.at[i]))
        copies[-1].start()
    for copy in copies:
        copy.wait()


def unpack(place, near, far, share, mems):
    memb_dev, rows, width_y = near[0].shape[-3:]
    vmem = pl.BlockSpec(memory_space=pltpu.VMEM)
    shape = (memb_dev, 2 * mems * rows, width_y)
    return pl.pallas_call(
        lambda *refs: unpack_kernel(share, mems, position(*place), *refs),
        in_specs=[vmem] * (2 * mems),
        out_specs=pl.BlockSpec(memory_space=pltpu.HBM),
        out_shape=jax.ShapeDtypeStruct(shape, F32),
        scratch_shapes=[pltpu.VMEM(shape, F32), pltpu.SemaphoreType.DMA((memb_dev,))],
        compiler_params=pltpu.CompilerParams(vmem_limit_bytes=VMEM_LIMIT),
        name="unpack",
    )(*[pltpu.with_memory_space_constraint(x, pltpu.VMEM) for x in (*near, *far)])


def along_tile(first, second):
    count = lax.axis_size("tile")

    def trade(value, start):
        pairs = []
        for i in range(start, count - 1, 2):
            pairs += [(i, i + 1), (i + 1, i)]
        return lax.ppermute(value, "tile", pairs)

    first = trade(first, 0)
    second = trade(second, 1)
    return first, second


def to_partner(value):
    return lax.ppermute(value, "section", [(0, 1), (1, 0)])


def over_mem(value, k):
    return lax.ppermute(value, "mem", [(i, i ^ k) for i in range(lax.axis_size("mem"))])


def across(value, k):
    size = lax.axis_size(GROUP)
    return lax.ppermute(value, GROUP, [(i, i ^ (size // 2) ^ k) for i in range(size)])


def analysis(state, speed_x, speed_y, diffuse, obs_cell, obs_value, obs_errinv, obs_list, obs_count):
    memb_dev, levels, width_x, _ = state.shape
    mems = lax.axis_size("mem")
    groups = lax.axis_size(GROUP)
    assert groups == 2 * mems and mems & (mems - 1) == 0
    tiles = lax.axis_size("tile")
    group_idx = lax.axis_index(GROUP)
    share = width_x // groups
    far = list(range(mems - 1, 0, -1))

    place = (tiles, width_x, share, mems)

    share_d = share // DB
    lists = lax.dynamic_slice_in_dim(obs_list, group_idx * share_d, share_d, 0)
    lists = lists.reshape(-1, obs_list.shape[2])
    counts = lax.dynamic_slice_in_dim(obs_count, group_idx * share_d, share_d, 0).reshape(-1, 1)

    a, b, info = pack(place, state, speed_x, speed_y, diffuse, obs_cell, obs_value, obs_errinv)
    a, b = along_tile(a, b)
    keep, send, own_obs = forecast(
        place, state, a, b, speed_x, speed_y, diffuse, obs_cell, share, mems
    )

    other_obs = to_partner(own_obs)
    other = to_partner(send)
    both_obs = jnp.stack([own_obs, other_obs])
    gathered = [both_obs] + [over_mem(both_obs, k) for k in far[::-1]]
    gathered = jnp.stack(gathered)
    joined = join(place, keep, other)
    near = []
    for k in far[::-1]:
        near.append(over_mem(joined[k - 1], k))
    near_a, near_b = along_tile(gathered, gathered)
    weight = weights(place, lists, counts, info, a, b, memb_dev * levels)
    part = own_gram(place, gathered, info, weight)
    inverse, mean = transforms(place, part, near_a, near_b, a, b, weight, memb_dev * levels)
    anomaly, base = centre(place, keep, other, near, mean)

    direct = None
    done, away = [None] * mems, [None] * mems
    for k in far + [0]:
        result = apply_transform(place, anomaly, base, inverse, mems, k, k == direct)
        done[k] = over_mem(result[0], k) if k else result[0]
        if k == direct:
            away[k] = across(result[1], k)
    for k in range(mems):
        if k != direct:
            away[k] = to_partner(done[k])
    return unpack(place, done, away, share, mems).reshape(state.shape)


def solution(mesh):
    placed = (
        P(GROUP, None, "tile", None),
        P(None, "tile", None),
        P(None, "tile", None),
        P("tile", None),
        P("tile"),
        P("tile"),
        P("tile"),
        P("tile", None, None),
        P("tile", None),
    )
    return jax.shard_map(
        analysis,
        mesh=mesh,
        in_specs=placed,
        out_specs=P(GROUP, None, "tile", None),
        check_vma=False,
    )
```

```python
import functools

import jax
import jax.numpy as jnp
from jax import lax
from jax.experimental import pallas as pl
from jax.experimental.pallas import tpu as pltpu
from jax.sharding import PartitionSpec as P

STEPS = 4
DB = 2
LOC = 4
LANES = 128
SUB = 8
LEVELS_AT_ONCE = 8
GROUP = ("section", "mem")
F32 = jnp.float32
BF16 = jnp.bfloat16
VMEM_LIMIT = 24 * 2**20


CENTRE, PARITY, SECTION, MEM, HAS_A, HAS_B, TILE_X = range(7)


def position(tiles, width_x, share, mems):
    tile, section, mem = (lax.axis_index(name) for name in ("tile", "section", "mem"))
    parity = tile % 2
    above, below = (tile < tiles - 1).astype(jnp.int32), (tile > 0).astype(jnp.int32)
    first = 2 * (tile * width_x + (section * mems + mem) * share) + DB - 1
    has_a = jnp.where(parity == 1, below, above)
    has_b = jnp.where(parity == 1, above, below)
    return first, parity, section, mem, has_a, has_b, tile * width_x


def call(kernel, outs, place, *args, scratch=(), inputs=pltpu.VMEM):
    vmem = pl.BlockSpec(memory_space=pltpu.VMEM)
    outs = [pltpu.VMEM(shape, dtype) for shape, dtype in outs]
    return pl.pallas_call(
        lambda *refs: kernel(position(*place), *refs),
        in_specs=[vmem] * len(args),
        out_specs=[vmem] * len(outs),
        out_shape=outs,
        scratch_shapes=list(scratch),
        compiler_params=pltpu.CompilerParams(vmem_limit_bytes=VMEM_LIMIT),
    )(*[pltpu.with_memory_space_constraint(a, inputs) for a in args])


def split_2(value):
    high = value.astype(BF16)
    return high, (value - high.astype(F32)).astype(BF16)


def pack_kernel(
    place_ref, state_ref, sx_ref, sy_ref, diff_ref, cell_ref, value_ref, err_ref, a_ref, b_ref, info_ref
):
    fields, width_x, width_y = state_ref.shape
    levels = sx_ref.shape[0]
    even = place_ref[PARITY] == 0
    cell = cell_ref[...]
    row = cell // width_y
    rows = cell.shape[0]
    info_ref[0:rows, :] = (place_ref[TILE_X] + row % width_x).astype(F32)
    info_ref[rows : 2 * rows, :] = (cell - row * width_y).astype(F32)
    info_ref[2 * rows : 3 * rows, :] = value_ref[...]
    info_ref[3 * rows : 4 * rows, :] = err_ref[...]
    at = lax.broadcasted_iota(jnp.int32, (STEPS, width_y), 0)

    def put(slot, values):
        low, high = values[:STEPS, :], values[width_x - STEPS :, :]
        extra = slot - fields
        if 0 <= extra < 4 * rows:
            line = info_ref[extra : extra + 1, :]
            low = jnp.where(at == STEPS - 1, line, low)
            high = jnp.where(at == 0, line, high)
        a_ref[slot] = jnp.where(even, high, low)
        b_ref[slot] = jnp.where(even, low, high)

    for i in range(fields):
        put(i, state_ref[i])
    for i in range(levels):
        put(fields + i, sx_ref[i])
        put(fields + levels + i, sy_ref[i])
    put(fields + 2 * levels, diff_ref[...])


def pack(place, state, speed_x, speed_y, diffuse, obs_cell, obs_value, obs_errinv):
    memb_dev, levels, width_x, width_y = state.shape
    fields = memb_dev * levels
    chunks = obs_cell.shape[0] // LANES
    slots = fields + 2 * levels + 1
    assert 4 * chunks <= 2 * levels + 1 and width_y == LANES
    return call(
        pack_kernel,
        [((slots, STEPS, width_y), F32), ((slots, STEPS, width_y), F32), ((4 * chunks, LANES), F32)],
        place,
        state.reshape(fields, width_x, width_y),
        speed_x,
        speed_y,
        diffuse,
        obs_cell.reshape(chunks, LANES),
        obs_value.reshape(chunks, LANES),
        obs_errinv.reshape(chunks, LANES),
        inputs=pltpu.HBM,
    )


def forecast_kernel(
    share,
    mems,
    place_ref,
    state_ref,
    a_ref,
    b_ref,
    sx_ref,
    sy_ref,
    diff_ref,
    cell_ref,
    keep_ref,
    send_ref,
    obs_ref,
    all_ref,
):
    fields, width_x, width_y = state_ref.shape
    levels = sx_ref.shape[0]
    memb_dev = fields // levels
    wide = width_x + 2 * STEPS
    even = place_ref[PARITY] == 0

    def ring(slot, own):
        first, second = a_ref[slot], b_ref[slot]
        above, below = jnp.where(even, first, second), jnp.where(even, second, first)
        return jnp.concatenate([own, above, below], axis=0)

    lane = lax.broadcasted_iota(jnp.int32, (wide, width_y), 1)
    diff = ring(fields + 2 * levels, diff_ref[...])
    at_once = LEVELS_AT_ONCE if levels % LEVELS_AT_ONCE == 0 else 1

    @pl.loop(0, levels // at_once)
    def _(block):
        coefs, fields_q = [], []
        for i in range(at_once):
            level = block * at_once + i
            sx = ring(fields + level, sx_ref[level])
            sy = ring(fields + levels + level, sy_ref[level])
            from_low = jnp.maximum(sx, 0.0) + diff
            from_high = diff - jnp.minimum(sx, 0.0)
            y_low = jnp.maximum(sy, 0.0) + diff
            y_high = diff - jnp.minimum(sy, 0.0)
            keep = 1.0 - (from_low + from_high + y_low + y_high)
            y_low = jnp.where(lane == 0, 0.0, y_low)
            y_high = jnp.where(lane == width_y - 1, 0.0, y_high)
            coefs.append((keep, from_low, from_high, y_low, y_high))
            fields_q.append(
                [ring(m * levels + level, state_ref[m * levels + level]) for m in range(memb_dev)]
            )
        for _ in range(STEPS):
            for i in range(at_once):
                keep, from_low, from_high, y_low, y_high = coefs[i]
                for member in range(memb_dev):
                    q = fields_q[i][member]
                    fields_q[i][member] = (
                        keep * q
                        + from_low * pltpu.roll(q, 1, 0)
                        + from_high * pltpu.roll(q, wide - 1, 0)
                        + y_low * pltpu.roll(q, 1, 1)
                        + y_high * pltpu.roll(q, width_y - 1, 1)
                    )
        for i in range(at_once):
            for member in range(memb_dev):
                at = pl.ds(pl.multiple_of((block * at_once + i) * width_x, SUB), width_x)
                all_ref[member, at, :] = fields_q[i][member][:width_x, :]

    for k in range(mems):
        for slot, part_ref in enumerate((keep_ref, send_ref)):
            group = (place_ref[SECTION] ^ slot) * mems + (place_ref[MEM] ^ k)
            for member in range(memb_dev):
                for row in range(share):
                    part_ref[k, member, pl.ds(row * levels, levels), :] = all_ref[
                        member, pl.ds(group * share + row, levels, stride=width_x), :
                    ]

    cell = cell_ref[...]
    obs = cell.shape[1]
    cell_row = cell // width_y
    cell_y = cell - cell_row * width_y
    rows = levels * width_x
    pick = (lax.broadcasted_iota(jnp.int32, (rows, obs), 0) == cell_row).astype(F32).astype(BF16)
    pick_y = lax.broadcasted_iota(jnp.int32, (width_y, obs), 0) == cell_y
    dims = (((0,), (0,)), ((), ()))
    for member in range(memb_dev):
        high, low = split_2(all_ref[member])
        found = lax.dot_general(high, pick, dims, preferred_element_type=F32)
        found = found + lax.dot_general(low, pick, dims, preferred_element_type=F32)
        obs_ref[pl.ds(member, 1), :] = jnp.sum(jnp.where(pick_y, found, 0.0), axis=0, keepdims=True)


def forecast(place, state, a, b, speed_x, speed_y, diffuse, obs_cell, share, mems):
    memb_dev, levels, width_x, width_y = state.shape
    fields = memb_dev * levels
    return call(
        functools.partial(forecast_kernel, share, mems),
        [((mems, memb_dev, share * levels, width_y), F32)] * 2 + [((memb_dev, obs_cell.shape[0]), F32)],
        place,
        state.reshape(fields, width_x, width_y),
        a,
        b,
        speed_x,
        speed_y,
        diffuse,
        obs_cell.reshape(1, -1),
        scratch=[
            pltpu.VMEM((memb_dev, levels * width_x, width_y), F32),
        ],
    )


def join_kernel(place_ref, keep_ref, other_ref, *out_refs):
    for k, out_ref in enumerate(out_refs):
        out_ref[0] = keep_ref[k + 1]
        out_ref[1] = other_ref[k + 1]


def join(place, keep, other):
    mems, *rest = keep.shape
    return call(join_kernel, [((2, *rest), F32)] * (mems - 1), place, keep, other)


def info_reader(place_ref, ref, fields, first):
    if fields is None:
        return lambda row: ref[row : row + 1, :]
    above = (place_ref[PARITY] == 0) == first

    def read(row):
        return jnp.where(above, ref[fields + row, STEPS - 1 :, :], ref[fields + row, 0:1, :])

    return read


def weight_kernel(fields, place_ref, list_ref, count_ref, own_ref, a_ref, b_ref, weight_ref):
    domains, slots = list_ref.shape
    chunks = own_ref.shape[0] // 4
    obs = chunks * LANES
    limit = float((8 * LOC) ** 2)
    slot = lax.broadcasted_iota(jnp.int32, (domains, slots), 1)
    last = jnp.sum(
        jnp.where(slot == count_ref[...] - 1, list_ref[...], 0).astype(F32), axis=1, keepdims=True
    )
    centre_x = place_ref[CENTRE].astype(F32)
    centre_y = lax.broadcasted_iota(jnp.int32, (domains, 1), 0).astype(F32) * (2.0 * DB) + (DB - 1.0)
    parity = place_ref[PARITY]
    sources = (
        (info_reader(place_ref, own_ref, None, None), 1, None),
        (info_reader(place_ref, a_ref, fields, True), 2 - 2 * parity, place_ref[HAS_A]),
        (info_reader(place_ref, b_ref, fields, False), 2 * parity, place_ref[HAS_B]),
    )

    def chunk_of(source, chunk):
        read, tile_slot, present = source
        delta_x = 2.0 * read(chunk) - centre_x
        delta_y = 2.0 * read(chunks + chunk) - centre_y
        dist = delta_x * delta_x + delta_y * delta_y
        inside = jnp.minimum(dist, limit)
        if present is not None:
            inside = jnp.where(present > 0, inside, limit)
        first = jnp.asarray(tile_slot * obs + chunk * LANES, jnp.int32)
        column = (lax.broadcasted_iota(jnp.int32, (1, LANES), 1) + first).astype(F32)
        return dist, inside * float(3 * obs) + column, column

    found = jnp.zeros((domains, LANES), F32)
    for source in sources:
        for chunk in range(chunks):
            _, score, column = chunk_of(source, chunk)
            found = found + jnp.where(column == last, score, 0.0)
    bound = jnp.sum(found, axis=1, keepdims=True)
    for n, source in enumerate(sources):
        for chunk in range(chunks):
            dist, score, _ = chunk_of(source, chunk)
            weight = source[0](3 * chunks + chunk) * jnp.exp(dist * (-1.0 / (8.0 * LOC * LOC)))
            high, low = split_2(jnp.where(score <= bound, weight, 0.0))
            at = pl.ds(n * obs + chunk * LANES, LANES)
            weight_ref[0:domains, at] = high
            weight_ref[domains : 2 * domains, at] = low


def weights(place, lists, counts, own, a, b, fields):
    domains = lists.shape[0]
    columns = 3 * (own.shape[0] // 4) * LANES
    kernel = functools.partial(weight_kernel, fields)
    return call(kernel, [((2 * domains, columns), BF16)], place, lists, counts, own, a, b)[0]


def pair_rows(members):
    starts = [SUB * (k // SUB) for k in range(members)]
    offsets, total = [], 0
    for start in starts:
        offsets.append(total)
        total += members - start
    return starts, offsets, total


def gram_of(place_ref, ens_ref, read, weight, y_ref, zh_ref, zl_ref):
    members, obs = y_ref.shape
    chunks = obs // LANES
    mems, _, memb_dev, _ = ens_ref.shape
    starts, offsets, total = pair_rows(members)
    for section in range(2):
        for mem in range(mems):
            rows = ens_ref[place_ref[MEM] ^ mem, place_ref[SECTION] ^ section]
            y_ref[pl.ds((section * mems + mem) * memb_dev, memb_dev), :] = rows
    ens = y_ref[...]
    ens_mean = jnp.mean(ens, axis=0, keepdims=True)
    y = ens - ens_mean
    y_ref[...] = y
    for k in range(0, members, 2):
        tail = y[starts[k] :, :]
        both = jnp.concatenate([tail * y_ref[k : k + 1, :], tail * y_ref[k + 1 : k + 2, :]], axis=0)
        high, low = split_2(both)
        zh_ref[pl.ds(offsets[k], both.shape[0]), :] = high
        zl_ref[pl.ds(offsets[k], both.shape[0]), :] = low
    value = jnp.concatenate([read(2 * chunks + c) for c in range(chunks)], axis=1)
    high, low = split_2(y * (value - ens_mean))
    zh_ref[pl.ds(total, members), :] = high
    zl_ref[pl.ds(total, members), :] = low
    dims = (((1,), (1,)), ((), ()))
    part = lax.dot_general(zh_ref[...], weight, dims, preferred_element_type=F32)
    return part + lax.dot_general(zl_ref[...], weight, dims, preferred_element_type=F32)


def gram_scratch(members, obs):
    _, _, total = pair_rows(members)
    return [
        pltpu.VMEM((members, obs), F32),
        pltpu.VMEM((total + members, obs), BF16),
        pltpu.VMEM((total + members, obs), BF16),
    ]


def own_gram_kernel(place_ref, own_ref, info_ref, weight_ref, out_ref, y_ref, zh_ref, zl_ref):
    read = info_reader(place_ref, info_ref, None, None)
    weight = weight_ref[:, 0 : y_ref.shape[1]]
    out_ref[...] = gram_of(place_ref, own_ref, read, weight, y_ref, zh_ref, zl_ref)


def ensemble(gathered):
    mems, sections, memb_dev, obs = gathered.shape
    return mems * sections * memb_dev, obs


def own_gram(place, own, info, weight):
    members, obs = ensemble(own)
    _, _, total = pair_rows(members)
    return call(
        own_gram_kernel,
        [((total + members, weight.shape[0]), F32)],
        place,
        own,
        info,
        weight,
        scratch=gram_scratch(members, obs),
    )[0]


def centre_kernel(place_ref, keep_ref, other_ref, *refs):
    near_refs, (mean_ref, anomaly_ref, base_ref) = refs[:-3], refs[-3:]
    members, rows, _ = anomaly_ref.shape
    mems = len(near_refs) + 1
    memb_dev = members // (2 * mems)

    def field_of(other, k, i, at):
        if k:
            return near_refs[k - 1][other, i, at, :]
        return other_ref[0, i, at, :] if other else keep_ref[0, i, at, :]

    for block in range(rows // SUB):
        at = pl.ds(block * SUB, SUB)
        fields = [
            (other, k, i, field_of(other, k, i, at))
            for other in range(2)
            for k in range(mems)
            for i in range(memb_dev)
        ]
        mean = sum(field for *_, field in fields) * (1.0 / members)
        base = mean
        for other, k, i, field in fields:
            member = ((place_ref[SECTION] ^ other) * mems + (place_ref[MEM] ^ k)) * memb_dev + i
            field = field - mean
            anomaly_ref[member, at, :] = field
            base = base + field * mean_ref[pl.ds(member, SUB, stride=0), :]
        base_ref[at, :] = base


def centre(place, keep, other, near, mean):
    mems, memb_dev, rows, width_y = keep.shape
    outs = [((2 * mems * memb_dev, rows, width_y), F32), ((rows, width_y), F32)]
    return call(centre_kernel, outs, place, keep, other, *near, mean)


def near_gram_kernel(fields, place_ref, part_ref, near_ref, info_ref, weight_ref, out_ref, *scratch):
    read = info_reader(place_ref, info_ref, fields, True)
    obs = near_ref.shape[3]
    weight = weight_ref[:, obs : 2 * obs]
    out_ref[...] = part_ref[...] + gram_of(place_ref, near_ref, read, weight, *scratch)


def near_gram(place, part, near, info, weight, fields):
    members, obs = ensemble(near)
    return call(
        functools.partial(near_gram_kernel, fields),
        [(part.shape, F32)],
        place,
        part,
        near,
        info,
        weight,
        scratch=gram_scratch(members, obs),
    )[0]


def transform_kernel(fields, place_ref, part_ref, near_ref, info_ref, weight_ref, *refs):
    inv_ref, mean_ref, y_ref, zh_ref, zl_ref, gram_ref, low_ref, s_ref = refs
    members, obs = y_ref.shape
    starts, offsets, total = pair_rows(members)
    read = info_reader(place_ref, info_ref, fields, False)
    weight = weight_ref[:, 2 * obs : 3 * obs]
    sums = part_ref[...] + gram_of(place_ref, near_ref, read, weight, y_ref, zh_ref, zl_ref)

    width = sums.shape[1]
    domain = lax.broadcasted_iota(jnp.int32, (width, LANES), 0) % (width // 2)
    column = lax.broadcasted_iota(jnp.int32, (width, LANES), 1) // DB
    spread = (domain == column).astype(F32).astype(BF16)
    high, low = split_2(sums)
    gram = jnp.dot(high, spread, preferred_element_type=F32)
    gram = gram + jnp.dot(low, spread, preferred_element_type=F32)
    gram_ref[...] = gram

    sub_row = lax.broadcasted_iota(jnp.int32, (SUB, LANES), 0)

    def every(ref, row):
        return ref[pl.ds(row, SUB, stride=0), :]

    blocks = members // SUB
    inv_ref[...] = jnp.zeros(inv_ref.shape, F32)
    mean = [jnp.zeros((SUB, LANES), F32) for _ in range(blocks)]
    for k in range(members):
        own = k // SUB
        acc = [gram_ref[pl.ds(offsets[k] - starts[k] + b * SUB, SUB), :] for b in range(own, blocks)]
        acc[0] = acc[0] + jnp.where(sub_row == k % SUB, members - 1.0, 0.0)
        inv = [jnp.zeros((SUB, LANES), F32) for _ in range(own)]
        inv.append(jnp.where(sub_row == k % SUB, 1.0, 0.0))
        forced = every(gram_ref, total + k)
        for j in range(k):
            base = offsets[j] - starts[j]
            factor = every(low_ref, base + k)
            for b in range(own, blocks):
                acc[b - own] = acc[b - own] - low_ref[pl.ds(base + b * SUB, SUB), :] * factor
            for b in range(j // SUB + 1):
                inv[b] = inv[b] - inv_ref[j, pl.ds(b * SUB, SUB), :] * factor
            forced = forced - s_ref[j] * factor
        pivot = jnp.broadcast_to(acc[0][k % SUB : k % SUB + 1, :], (SUB, LANES))
        scale = lax.rsqrt(pivot)
        scale = scale * (1.5 - 0.5 * pivot * scale * scale)
        for b in range(own, blocks):
            low_ref[pl.ds(offsets[k] - starts[k] + b * SUB, SUB), :] = acc[b - own] * scale
        forced = forced * scale
        s_ref[k] = forced
        for b in range(own + 1):
            inv[b] = inv[b] * scale
            inv_ref[k, pl.ds(b * SUB, SUB), :] = inv[b]
            mean[b] = mean[b] + inv[b] * forced
    for b in range(blocks):
        mean_ref[pl.ds(b * SUB, SUB), :] = mean[b]


def transforms(place, part, near, info, weight, fields):
    members, obs = ensemble(near)
    _, _, total = pair_rows(members)
    return call(
        functools.partial(transform_kernel, fields),
        [((members, members, LANES), F32), ((members, LANES), F32)],
        place,
        part,
        near,
        info,
        weight,
        scratch=gram_scratch(members, obs)
        + [
            pltpu.VMEM((total + members, LANES), F32),
            pltpu.VMEM((total, LANES), F32),
            pltpu.VMEM((members, SUB, LANES), F32),
        ],
    )


def apply_kernel(mems, k, place_ref, anomaly_ref, base_ref, inv_ref, *out_refs):
    members, rows, _ = anomaly_ref.shape
    memb_dev = members // (2 * mems)
    root = float(members - 1) ** 0.5
    blocks = rows // SUB
    if len(out_refs) == 1:
        out_refs = [out_refs[0].at[slot] for slot in range(2)]
    for slot in range(2):
        group = (place_ref[SECTION] ^ slot) * mems + (place_ref[MEM] ^ k)
        first = group * memb_dev
        zero = tuple(jnp.zeros((SUB, LANES), F32) for _ in range(memb_dev * blocks))

        def step(chunk, acc, first=first):
            acc = list(acc)
            for t in range(memb_dev):
                j = chunk * memb_dev + t
                fields = [anomaly_ref[j, pl.ds(b * SUB, SUB), :] for b in range(blocks)]
                for i in range(memb_dev):
                    factor = inv_ref[first + i, pl.ds(j, SUB, stride=0), :]
                    for b in range(blocks):
                        acc[i * blocks + b] = acc[i * blocks + b] + fields[b] * factor
            return tuple(acc)

        acc = lax.fori_loop(0, group + 1, step, zero)
        for i in range(memb_dev):
            for b in range(blocks):
                at = pl.ds(b * SUB, SUB)
                out_refs[slot][i, at, :] = base_ref[at, :] + root * acc[i * blocks + b]


def apply_transform(place, anomaly, base, inverse, mems, k, split):
    members, rows, width_y = anomaly.shape
    block = (members // (2 * mems), rows, width_y)
    outs = [(block, F32)] * 2 if split else [((2, *block), F32)]
    return call(functools.partial(apply_kernel, mems, k), outs, place, anomaly, base, inverse)


def unpack_kernel(share, mems, place_ref, *refs):
    near_refs, far_refs, (out_ref, all_ref, sem_ref) = refs[:mems], refs[mems : 2 * mems], refs[2 * mems :]
    memb_dev, total, _ = all_ref.shape
    levels = total // (2 * mems * share)
    width_x = total // levels
    copies = []
    for i in range(memb_dev):
        for other in range(2):
            for k in range(mems):
                group = (place_ref[SECTION] ^ other) * mems + (place_ref[MEM] ^ k)
                block_ref = (far_refs if other else near_refs)[k]
                if len(block_ref.shape) == 4:
                    block_ref = block_ref.at[other]
                for row in range(share):
                    all_ref[i, pl.ds(group * share + row, levels, stride=width_x), :] = block_ref[
                        i, pl.ds(row * levels, levels), :
                    ]
        copies.append(pltpu.make_async_copy(all_ref.at[i], out_ref.at[i], sem_ref.at[i]))
        copies[-1].start()
    for copy in copies:
        copy.wait()


def unpack(place, near, far, share, mems):
    memb_dev, rows, width_y = near[0].shape[-3:]
    vmem = pl.BlockSpec(memory_space=pltpu.VMEM)
    shape = (memb_dev, 2 * mems * rows, width_y)
    return pl.pallas_call(
        lambda *refs: unpack_kernel(share, mems, position(*place), *refs),
        in_specs=[vmem] * (2 * mems),
        out_specs=pl.BlockSpec(memory_space=pltpu.HBM),
        out_shape=jax.ShapeDtypeStruct(shape, F32),
        scratch_shapes=[pltpu.VMEM(shape, F32), pltpu.SemaphoreType.DMA((memb_dev,))],
        compiler_params=pltpu.CompilerParams(vmem_limit_bytes=VMEM_LIMIT),
        name="unpack",
    )(*[pltpu.with_memory_space_constraint(x, pltpu.VMEM) for x in (*near, *far)])


def along_tile(first, second):
    count = lax.axis_size("tile")

    def trade(value, start):
        pairs = []
        for i in range(start, count - 1, 2):
            pairs += [(i, i + 1), (i + 1, i)]
        return lax.ppermute(value, "tile", pairs)

    first = trade(first, 0)
    second = trade(second, 1)
    return first, second


def to_partner(value):
    return lax.ppermute(value, "section", [(0, 1), (1, 0)])


def over_mem(value, k):
    return lax.ppermute(value, "mem", [(i, i ^ k) for i in range(lax.axis_size("mem"))])


def across(value, k):
    size = lax.axis_size(GROUP)
    return lax.ppermute(value, GROUP, [(i, i ^ (size // 2) ^ k) for i in range(size)])


def analysis(state, speed_x, speed_y, diffuse, obs_cell, obs_value, obs_errinv, obs_list, obs_count):
    memb_dev, levels, width_x, _ = state.shape
    mems = lax.axis_size("mem")
    groups = lax.axis_size(GROUP)
    assert groups == 2 * mems and mems & (mems - 1) == 0
    tiles = lax.axis_size("tile")
    group_idx = lax.axis_index(GROUP)
    share = width_x // groups
    far = list(range(mems - 1, 0, -1))

    place = (tiles, width_x, share, mems)

    share_d = share // DB
    lists = lax.dynamic_slice_in_dim(obs_list, group_idx * share_d, share_d, 0)
    lists = lists.reshape(-1, obs_list.shape[2])
    counts = lax.dynamic_slice_in_dim(obs_count, group_idx * share_d, share_d, 0).reshape(-1, 1)

    a, b, info = pack(place, state, speed_x, speed_y, diffuse, obs_cell, obs_value, obs_errinv)
    a, b = along_tile(a, b)
    keep, send, own_obs = forecast(
        place, state, a, b, speed_x, speed_y, diffuse, obs_cell, share, mems
    )

    other_obs = to_partner(own_obs)
    other = to_partner(send)
    both_obs = jnp.stack([own_obs, other_obs])
    gathered = [both_obs]
    for k in far[::-1]:
        gathered.append(over_mem(both_obs, k))
    gathered = jnp.stack(gathered)
    joined = join(place, keep, other)
    near = []
    for k in far[::-1]:
        near.append(over_mem(joined[k - 1], k))
    near_a, near_b = along_tile(gathered, gathered)
    weight = weights(place, lists, counts, info, a, b, memb_dev * levels)
    part = own_gram(place, gathered, info, weight)
    part = near_gram(place, part, near_a, a, weight, memb_dev * levels)
    inverse, mean = transforms(place, part, near_b, b, weight, memb_dev * levels)
    anomaly, base = centre(place, keep, other, near, mean)

    direct = None
    done, away = [None] * mems, [None] * mems
    for k in far + [0]:
        result = apply_transform(place, anomaly, base, inverse, mems, k, k == direct)
        done[k] = over_mem(result[0], k) if k else result[0]
        if k == direct:
            away[k] = across(result[1], k)
    for k in range(mems):
        if k != direct:
            away[k] = to_partner(done[k])
    return unpack(place, done, away, share, mems).reshape(state.shape)


def solution(mesh):
    placed = (
        P(GROUP, None, "tile", None),
        P(None, "tile", None),
        P(None, "tile", None),
        P("tile", None),
        P("tile"),
        P("tile"),
        P("tile"),
        P("tile", None, None),
        P("tile", None),
    )
    return jax.shard_map(
        analysis,
        mesh=mesh,
        in_specs=placed,
        out_specs=P(GROUP, None, "tile", None),
        check_vma=False,
    )
```

```python
import functools

import jax
import jax.numpy as jnp
from jax import lax
from jax.experimental import pallas as pl
from jax.experimental.pallas import tpu as pltpu
from jax.sharding import PartitionSpec as P

STEPS = 4
DB = 2
LOC = 4
LANES = 128
SUB = 8
LEVELS_AT_ONCE = 16
GROUP = ("section", "mem")
F32 = jnp.float32
BF16 = jnp.bfloat16
ROWS = (((0,), (0,)), ((), ()))
VMEM_LIMIT = 24 * 2**20


CENTRE, PARITY, SECTION, MEM, HAS_A, HAS_B, TILE_X = range(7)


def position(tiles, width_x, share, mems):
    tile, section, mem = (lax.axis_index(name) for name in ("tile", "section", "mem"))
    parity = tile % 2
    above, below = (tile < tiles - 1).astype(jnp.int32), (tile > 0).astype(jnp.int32)
    first = 2 * (tile * width_x + (section * mems + mem) * share) + DB - 1
    has_a = jnp.where(parity == 1, below, above)
    has_b = jnp.where(parity == 1, above, below)
    return first, parity, section, mem, has_a, has_b, tile * width_x


def call(kernel, outs, place, *args, scratch=(), inputs=pltpu.VMEM):
    vmem = pl.BlockSpec(memory_space=pltpu.VMEM)
    outs = [pltpu.VMEM(shape, dtype) for shape, dtype in outs]
    return pl.pallas_call(
        lambda *refs: kernel(position(*place), *refs),
        in_specs=[vmem] * len(args),
        out_specs=[vmem] * len(outs),
        out_shape=outs,
        scratch_shapes=list(scratch),
        compiler_params=pltpu.CompilerParams(vmem_limit_bytes=VMEM_LIMIT),
    )(*[pltpu.with_memory_space_constraint(a, inputs) for a in args])


def split_2(value):
    high = value.astype(BF16)
    return high, (value - high.astype(F32)).astype(BF16)


def pack_kernel(
    place_ref,
    state_hbm,
    sx_hbm,
    sy_hbm,
    diff_hbm,
    cell_hbm,
    value_hbm,
    err_hbm,
    a_ref,
    b_ref,
    info_ref,
    state_ref,
    sx_ref,
    sy_ref,
    diff_ref,
    cell_ref,
    value_ref,
    err_ref,
    sem_ref,
):
    moves = [
        pltpu.make_async_copy(source, target, sem_ref.at[n])
        for n, (source, target) in enumerate(
            (
                (state_hbm, state_ref),
                (sx_hbm, sx_ref),
                (sy_hbm, sy_ref),
                (diff_hbm, diff_ref),
                (cell_hbm, cell_ref),
                (value_hbm, value_ref),
                (err_hbm, err_ref),
            )
        )
    ]
    for move in moves:
        move.start()
    for move in moves[1:]:
        move.wait()
    fields, width_x, width_y = state_ref.shape
    levels = sx_ref.shape[0]
    even = place_ref[PARITY] == 0
    cell = cell_ref[...]
    row = cell // width_y
    rows = cell.shape[0]
    info_ref[0:rows, :] = (place_ref[TILE_X] + row % width_x).astype(F32)
    info_ref[rows : 2 * rows, :] = (cell - row * width_y).astype(F32)
    info_ref[2 * rows : 3 * rows, :] = value_ref[...]
    info_ref[3 * rows : 4 * rows, :] = err_ref[...]
    at = lax.broadcasted_iota(jnp.int32, (STEPS, width_y), 0)

    def put(slot, values):
        low, high = values[:STEPS, :], values[width_x - STEPS :, :]
        extra = slot - fields
        if 0 <= extra < 4 * rows:
            line = info_ref[extra : extra + 1, :]
            low = jnp.where(at == STEPS - 1, line, low)
            high = jnp.where(at == 0, line, high)
        a_ref[slot] = jnp.where(even, high, low)
        b_ref[slot] = jnp.where(even, low, high)

    for i in range(levels):
        put(fields + i, sx_ref[i])
        put(fields + levels + i, sy_ref[i])
    put(fields + 2 * levels, diff_ref[...])
    moves[0].wait()
    for i in range(fields):
        put(i, state_ref[i])


def pack(place, state, speed_x, speed_y, diffuse, obs_cell, obs_value, obs_errinv):
    memb_dev, levels, width_x, width_y = state.shape
    fields = memb_dev * levels
    chunks = obs_cell.shape[0] // LANES
    slots = fields + 2 * levels + 1
    assert 4 * chunks <= 2 * levels + 1 and width_y == LANES
    wide = (chunks, LANES)
    args = (
        state.reshape(fields, width_x, width_y),
        speed_x,
        speed_y,
        diffuse,
        obs_cell.reshape(wide),
        obs_value.reshape(wide),
        obs_errinv.reshape(wide),
    )
    vmem = pl.BlockSpec(memory_space=pltpu.VMEM)
    outs = [(slots, STEPS, width_y), (slots, STEPS, width_y), (4 * chunks, LANES)]
    outs += [x.shape for x in args[:4]]
    return pl.pallas_call(
        lambda *refs: pack_kernel(position(*place), *refs),
        in_specs=[pl.BlockSpec(memory_space=pltpu.HBM)] * len(args),
        out_specs=[vmem] * len(outs),
        out_shape=[pltpu.VMEM(shape, F32) for shape in outs],
        scratch_shapes=[
            pltpu.VMEM(wide, jnp.int32),
            pltpu.VMEM(wide, F32),
            pltpu.VMEM(wide, F32),
            pltpu.SemaphoreType.DMA((len(args),)),
        ],
        compiler_params=pltpu.CompilerParams(vmem_limit_bytes=VMEM_LIMIT),
        name="pack",
    )(*[pltpu.with_memory_space_constraint(x, pltpu.HBM) for x in args])


def coefficients(sx, sy, diff):
    lane = lax.broadcasted_iota(jnp.int32, sx.shape, 1)
    from_low = jnp.maximum(sx, 0.0) + diff
    from_high = diff - jnp.minimum(sx, 0.0)
    y_low = jnp.maximum(sy, 0.0) + diff
    y_high = diff - jnp.minimum(sy, 0.0)
    keep = 1.0 - (from_low + from_high + y_low + y_high)
    y_low = jnp.where(lane == 0, 0.0, y_low)
    y_high = jnp.where(lane == sx.shape[1] - 1, 0.0, y_high)
    return keep, from_low, from_high, y_low, y_high


def advance(q, q_low, q_high, coefs):
    keep, from_low, from_high, y_low, y_high = coefs
    return (
        keep * q
        + from_low * q_low
        + from_high * q_high
        + y_low * pltpu.roll(q, 1, 1)
        + y_high * pltpu.roll(q, q.shape[1] - 1, 1)
    )


def levels_at_once(levels):
    return LEVELS_AT_ONCE if levels % LEVELS_AT_ONCE == 0 else 1


def interior_kernel(place_ref, state_ref, sx_ref, sy_ref, diff_ref, cell_ref, mid_ref, side_ref, pick_ref, obs_ref):
    fields, width_x, width_y = state_ref.shape
    levels = sx_ref.shape[0]
    memb_dev = fields // levels
    at_once = levels_at_once(levels)
    diff = diff_ref[...]
    inner, outer = STEPS, width_x - 1 - STEPS

    @pl.loop(0, levels // at_once)
    def _(block):
        first = block * at_once
        coefs = [coefficients(sx_ref[first + i], sy_ref[first + i], diff) for i in range(at_once)]
        slots = [[m * levels + first + i for m in range(memb_dev)] for i in range(at_once)]
        fields_q = [[state_ref[slot] for slot in row] for row in slots]
        for step in range(STEPS):
            for i in range(at_once):
                for m in range(memb_dev):
                    q = fields_q[i][m]
                    side_ref[slots[i][m], step : step + 1, :] = q[inner : inner + 1, :]
                    side_ref[slots[i][m], STEPS + step : STEPS + step + 1, :] = q[outer : outer + 1, :]
                    fields_q[i][m] = advance(
                        q, pltpu.roll(q, 1, 0), pltpu.roll(q, width_x - 1, 0), coefs[i]
                    )
        for i in range(at_once):
            for m in range(memb_dev):
                mid_ref[slots[i][m]] = fields_q[i][m]

    cell = cell_ref[...]
    obs = cell.shape[1]
    cell_row = cell // width_y
    level, row = cell_row // width_x, cell_row % width_x
    inside = (row >= STEPS) & (row < width_x - STEPS)
    wanted = jnp.where(inside, cell_row, -1)
    shape = (levels * width_x, obs)
    pick = (lax.broadcasted_iota(jnp.int32, shape, 0) == wanted).astype(F32).astype(BF16)
    pick_y = lax.broadcasted_iota(jnp.int32, (width_y, obs), 0) == cell - cell_row * width_y
    for m in range(memb_dev):
        high, low = split_2(mid_ref[m * levels : (m + 1) * levels].reshape(levels * width_x, width_y))
        found = lax.dot_general(high, pick, ROWS, preferred_element_type=F32)
        found = found + lax.dot_general(low, pick, ROWS, preferred_element_type=F32)
        obs_ref[m : m + 1, :] = jnp.sum(jnp.where(pick_y, found, 0.0), axis=0, keepdims=True)

    edge = jnp.where(row < STEPS, row, row - (width_x - 2 * STEPS))
    wanted = jnp.where(inside, -1, level * (2 * STEPS) + edge)
    half = levels * 2 * STEPS
    pick = (lax.broadcasted_iota(jnp.int32, (half, obs), 0) == wanted).astype(F32).astype(BF16)
    pick_ref[0:half, :] = pick
    pick_ref[half : 2 * half, :] = pick


def interior(place, state, speed_x, speed_y, diffuse, obs_cell):
    memb_dev, levels, width_x, width_y = state.shape
    fields = memb_dev * levels
    assert STEPS * 2 == SUB and width_x == 2 * SUB
    return call(
        interior_kernel,
        [
            ((fields, width_x, width_y), F32),
            ((fields, 2 * STEPS, width_y), F32),
            ((levels * 4 * STEPS, obs_cell.shape[0]), BF16),
            ((memb_dev, obs_cell.shape[0]), F32),
        ],
        place,
        state.reshape(fields, width_x, width_y),
        speed_x,
        speed_y,
        diffuse,
        obs_cell.reshape(1, -1),
    )


def forecast_kernel(
    share,
    mems,
    place_ref,
    state_ref,
    a_ref,
    b_ref,
    sx_ref,
    sy_ref,
    diff_ref,
    cell_ref,
    mid_ref,
    side_ref,
    pick_ref,
    inner_obs_ref,
    keep_ref,
    send_ref,
    obs_ref,
    all_ref,
    edge_ref,
):
    fields, width_x, width_y = state_ref.shape
    levels = sx_ref.shape[0]
    memb_dev = fields // levels
    even = place_ref[PARITY] == 0
    sub_row = lax.broadcasted_iota(jnp.int32, (SUB, width_y), 0)

    def edges(slot, own):
        first, second = a_ref[slot], b_ref[slot]
        above, below = jnp.where(even, first, second), jnp.where(even, second, first)
        return jnp.concatenate([below, own[:STEPS, :], own[width_x - STEPS :, :], above], axis=0)

    diff = edges(fields + 2 * levels, diff_ref[...])
    at_once = levels_at_once(levels)

    @pl.loop(0, levels // at_once)
    def _(block):
        first = block * at_once
        coefs, fields_q = [], []
        for i in range(at_once):
            level = first + i
            sx = edges(fields + level, sx_ref[level])
            sy = edges(fields + levels + level, sy_ref[level])
            coefs.append(coefficients(sx, sy, diff))
            fields_q.append(
                [edges(m * levels + level, state_ref[m * levels + level]) for m in range(memb_dev)]
            )
        for step in range(STEPS):
            for i in range(at_once):
                for m in range(memb_dev):
                    q = fields_q[i][m]
                    slot = m * levels + first + i
                    low, high = q[:SUB, :], q[SUB:, :]
                    past_low = jnp.where(
                        sub_row == SUB - 1, side_ref[slot, step : step + 1, :], pltpu.roll(low, SUB - 1, 0)
                    )
                    past_high = jnp.where(
                        sub_row == 0,
                        side_ref[slot, STEPS + step : STEPS + step + 1, :],
                        pltpu.roll(high, 1, 0),
                    )
                    q_low = jnp.concatenate([pltpu.roll(low, 1, 0), past_high], axis=0)
                    q_high = jnp.concatenate([past_low, pltpu.roll(high, SUB - 1, 0)], axis=0)
                    fields_q[i][m] = advance(q, q_low, q_high, coefs[i])
        for i in range(at_once):
            for m in range(memb_dev):
                q, mid = fields_q[i][m], mid_ref[m * levels + first + i]
                low, high = pltpu.roll(q[:SUB, :], STEPS, 0), pltpu.roll(q[SUB:, :], STEPS, 0)
                at = pl.multiple_of((first + i) * width_x, SUB)
                all_ref[m, pl.ds(at, SUB), :] = jnp.where(sub_row < STEPS, low, mid[:SUB, :])
                all_ref[m, pl.ds(at + SUB, SUB), :] = jnp.where(sub_row < STEPS, mid[SUB:, :], high)
                at = pl.multiple_of((first + i) * SUB, SUB)
                edge_ref[m, pl.ds(at, SUB), :] = jnp.where(sub_row < STEPS, low, high)

    for k in range(mems):
        for slot, part_ref in enumerate((keep_ref, send_ref)):
            group = (place_ref[SECTION] ^ slot) * mems + (place_ref[MEM] ^ k)
            for member in range(memb_dev):
                for row in range(share):
                    part_ref[k, member, pl.ds(row * levels, levels), :] = all_ref[
                        member, pl.ds(group * share + row, levels, stride=width_x), :
                    ]

    cell = cell_ref[...]
    obs = cell.shape[1]
    pick_y = lax.broadcasted_iota(jnp.int32, (width_y, obs), 0) == cell % width_y
    for m in range(memb_dev):
        both = jnp.concatenate(split_2(edge_ref[m]), axis=0)
        found = lax.dot_general(both, pick_ref[...], ROWS, preferred_element_type=F32)
        found = jnp.sum(jnp.where(pick_y, found, 0.0), axis=0, keepdims=True)
        obs_ref[m : m + 1, :] = inner_obs_ref[m : m + 1, :] + found


def forecast(place, state, a, b, speed_x, speed_y, diffuse, obs_cell, inner, share, mems):
    memb_dev, levels, width_x, width_y = state.shape
    fields = memb_dev * levels
    return call(
        functools.partial(forecast_kernel, share, mems),
        [((mems, memb_dev, share * levels, width_y), F32)] * 2 + [((memb_dev, obs_cell.shape[0]), F32)],
        place,
        state.reshape(fields, width_x, width_y),
        a,
        b,
        speed_x,
        speed_y,
        diffuse,
        obs_cell.reshape(1, -1),
        *inner,
        scratch=[
            pltpu.VMEM((memb_dev, levels * width_x, width_y), F32),
            pltpu.VMEM((memb_dev, levels * SUB, width_y), F32),
        ],
    )


def join_kernel(place_ref, keep_ref, other_ref, *out_refs):
    for k, out_ref in enumerate(out_refs):
        out_ref[0] = keep_ref[k + 1]
        out_ref[1] = other_ref[k + 1]


def join(place, keep, other):
    mems, *rest = keep.shape
    return call(join_kernel, [((2, *rest), F32)] * (mems - 1), place, keep, other)


def info_reader(place_ref, ref, fields, first):
    if fields is None:
        return lambda row: ref[row : row + 1, :]
    above = (place_ref[PARITY] == 0) == first

    def read(row):
        return jnp.where(above, ref[fields + row, STEPS - 1 :, :], ref[fields + row, 0:1, :])

    return read


def weight_kernel(fields, place_ref, list_ref, count_ref, own_ref, a_ref, b_ref, weight_ref):
    domains, slots = list_ref.shape
    chunks = own_ref.shape[0] // 4
    obs = chunks * LANES
    limit = float((8 * LOC) ** 2)
    slot = lax.broadcasted_iota(jnp.int32, (domains, slots), 1)
    last = jnp.sum(
        jnp.where(slot == count_ref[...] - 1, list_ref[...], 0).astype(F32), axis=1, keepdims=True
    )
    centre_x = place_ref[CENTRE].astype(F32)
    centre_y = lax.broadcasted_iota(jnp.int32, (domains, 1), 0).astype(F32) * (2.0 * DB) + (DB - 1.0)
    parity = place_ref[PARITY]
    sources = (
        (info_reader(place_ref, own_ref, None, None), 1, None),
        (info_reader(place_ref, a_ref, fields, True), 2 - 2 * parity, place_ref[HAS_A]),
        (info_reader(place_ref, b_ref, fields, False), 2 * parity, place_ref[HAS_B]),
    )

    def chunk_of(source, chunk):
        read, tile_slot, present = source
        delta_x = 2.0 * read(chunk) - centre_x
        delta_y = 2.0 * read(chunks + chunk) - centre_y
        dist = delta_x * delta_x + delta_y * delta_y
        inside = jnp.minimum(dist, limit)
        if present is not None:
            inside = jnp.where(present > 0, inside, limit)
        first = jnp.asarray(tile_slot * obs + chunk * LANES, jnp.int32)
        column = (lax.broadcasted_iota(jnp.int32, (1, LANES), 1) + first).astype(F32)
        return dist, inside * float(3 * obs) + column, column

    found = jnp.zeros((domains, LANES), F32)
    for source in sources:
        for chunk in range(chunks):
            _, score, column = chunk_of(source, chunk)
            found = found + jnp.where(column == last, score, 0.0)
    bound = jnp.sum(found, axis=1, keepdims=True)
    for n, source in enumerate(sources):
        for chunk in range(chunks):
            dist, score, _ = chunk_of(source, chunk)
            weight = source[0](3 * chunks + chunk) * jnp.exp(dist * (-1.0 / (8.0 * LOC * LOC)))
            high, low = split_2(jnp.where(score <= bound, weight, 0.0))
            at = pl.ds(n * obs + chunk * LANES, LANES)
            weight_ref[0:domains, at] = high
            weight_ref[domains : 2 * domains, at] = low


def weights(place, lists, counts, own, a, b, fields):
    domains = lists.shape[0]
    columns = 3 * (own.shape[0] // 4) * LANES
    kernel = functools.partial(weight_kernel, fields)
    return call(kernel, [((2 * domains, columns), BF16)], place, lists, counts, own, a, b)[0]


def pair_rows(members):
    starts = [SUB * (k // SUB) for k in range(members)]
    offsets, total = [], 0
    for start in starts:
        offsets.append(total)
        total += members - start
    return starts, offsets, total


def gram_of(place_ref, ens_ref, read, weight, y_ref, zh_ref, zl_ref):
    members, obs = y_ref.shape
    chunks = obs // LANES
    mems, _, memb_dev, _ = ens_ref.shape
    starts, offsets, total = pair_rows(members)
    for section in range(2):
        for mem in range(mems):
            rows = ens_ref[place_ref[MEM] ^ mem, place_ref[SECTION] ^ section]
            y_ref[pl.ds((section * mems + mem) * memb_dev, memb_dev), :] = rows
    ens = y_ref[...]
    ens_mean = jnp.mean(ens, axis=0, keepdims=True)
    y = ens - ens_mean
    y_ref[...] = y
    for k in range(0, members, 2):
        tail = y[starts[k] :, :]
        both = jnp.concatenate([tail * y_ref[k : k + 1, :], tail * y_ref[k + 1 : k + 2, :]], axis=0)
        high, low = split_2(both)
        zh_ref[pl.ds(offsets[k], both.shape[0]), :] = high
        zl_ref[pl.ds(offsets[k], both.shape[0]), :] = low
    value = jnp.concatenate([read(2 * chunks + c) for c in range(chunks)], axis=1)
    high, low = split_2(y * (value - ens_mean))
    zh_ref[pl.ds(total, members), :] = high
    zl_ref[pl.ds(total, members), :] = low
    dims = (((1,), (1,)), ((), ()))
    part = lax.dot_general(zh_ref[...], weight, dims, preferred_element_type=F32)
    return part + lax.dot_general(zl_ref[...], weight, dims, preferred_element_type=F32)


def gram_scratch(members, obs):
    _, _, total = pair_rows(members)
    return [
        pltpu.VMEM((members, obs), F32),
        pltpu.VMEM((total + members, obs), BF16),
        pltpu.VMEM((total + members, obs), BF16),
    ]


def own_gram_kernel(place_ref, own_ref, info_ref, weight_ref, out_ref, y_ref, zh_ref, zl_ref):
    read = info_reader(place_ref, info_ref, None, None)
    weight = weight_ref[:, 0 : y_ref.shape[1]]
    out_ref[...] = gram_of(place_ref, own_ref, read, weight, y_ref, zh_ref, zl_ref)


def ensemble(gathered):
    mems, sections, memb_dev, obs = gathered.shape
    return mems * sections * memb_dev, obs


def own_gram(place, own, info, weight):
    members, obs = ensemble(own)
    _, _, total = pair_rows(members)
    return call(
        own_gram_kernel,
        [((total + members, weight.shape[0]), F32)],
        place,
        own,
        info,
        weight,
        scratch=gram_scratch(members, obs),
    )[0]


def centre_kernel(place_ref, keep_ref, other_ref, *refs):
    near_refs, (mean_ref, anomaly_ref, base_ref) = refs[:-3], refs[-3:]
    members, rows, _ = anomaly_ref.shape
    mems = len(near_refs) + 1
    memb_dev = members // (2 * mems)

    def field_of(other, k, i, at):
        if k:
            return near_refs[k - 1][other, i, at, :]
        return other_ref[0, i, at, :] if other else keep_ref[0, i, at, :]

    for block in range(rows // SUB):
        at = pl.ds(block * SUB, SUB)
        fields = [
            (other, k, i, field_of(other, k, i, at))
            for other in range(2)
            for k in range(mems)
            for i in range(memb_dev)
        ]
        mean = sum(field for *_, field in fields) * (1.0 / members)
        base = mean
        for other, k, i, field in fields:
            member = ((place_ref[SECTION] ^ other) * mems + (place_ref[MEM] ^ k)) * memb_dev + i
            field = field - mean
            anomaly_ref[member, at, :] = field
            base = base + field * mean_ref[pl.ds(member, SUB, stride=0), :]
        base_ref[at, :] = base


def centre(place, keep, other, near, mean):
    mems, memb_dev, rows, width_y = keep.shape
    outs = [((2 * mems * memb_dev, rows, width_y), F32), ((rows, width_y), F32)]
    return call(centre_kernel, outs, place, keep, other, *near, mean)


def near_gram_kernel(fields, place_ref, part_ref, near_ref, info_ref, weight_ref, out_ref, *scratch):
    read = info_reader(place_ref, info_ref, fields, True)
    obs = near_ref.shape[3]
    weight = weight_ref[:, obs : 2 * obs]
    out_ref[...] = part_ref[...] + gram_of(place_ref, near_ref, read, weight, *scratch)


def near_gram(place, part, near, info, weight, fields):
    members, obs = ensemble(near)
    return call(
        functools.partial(near_gram_kernel, fields),
        [(part.shape, F32)],
        place,
        part,
        near,
        info,
        weight,
        scratch=gram_scratch(members, obs),
    )[0]


def transform_kernel(fields, place_ref, part_ref, near_ref, info_ref, weight_ref, *refs):
    inv_ref, mean_ref, y_ref, zh_ref, zl_ref, gram_ref, low_ref, s_ref = refs
    members, obs = y_ref.shape
    starts, offsets, total = pair_rows(members)
    read = info_reader(place_ref, info_ref, fields, False)
    weight = weight_ref[:, 2 * obs : 3 * obs]
    sums = part_ref[...] + gram_of(place_ref, near_ref, read, weight, y_ref, zh_ref, zl_ref)

    width = sums.shape[1]
    domain = lax.broadcasted_iota(jnp.int32, (width, LANES), 0) % (width // 2)
    column = lax.broadcasted_iota(jnp.int32, (width, LANES), 1) // DB
    spread = (domain == column).astype(F32).astype(BF16)
    high, low = split_2(sums)
    gram = jnp.dot(high, spread, preferred_element_type=F32)
    gram = gram + jnp.dot(low, spread, preferred_element_type=F32)
    gram_ref[...] = gram

    sub_row = lax.broadcasted_iota(jnp.int32, (SUB, LANES), 0)

    def every(ref, row):
        return ref[pl.ds(row, SUB, stride=0), :]

    blocks = members // SUB
    inv_ref[...] = jnp.zeros(inv_ref.shape, F32)
    mean = [jnp.zeros((SUB, LANES), F32) for _ in range(blocks)]
    for k in range(members):
        own = k // SUB
        acc = [gram_ref[pl.ds(offsets[k] - starts[k] + b * SUB, SUB), :] for b in range(own, blocks)]
        acc[0] = acc[0] + jnp.where(sub_row == k % SUB, members - 1.0, 0.0)
        inv = [jnp.zeros((SUB, LANES), F32) for _ in range(own)]
        inv.append(jnp.where(sub_row == k % SUB, 1.0, 0.0))
        forced = every(gram_ref, total + k)
        for j in range(k):
            base = offsets[j] - starts[j]
            factor = every(low_ref, base + k)
            for b in range(own, blocks):
                acc[b - own] = acc[b - own] - low_ref[pl.ds(base + b * SUB, SUB), :] * factor
            for b in range(j // SUB + 1):
                inv[b] = inv[b] - inv_ref[j, pl.ds(b * SUB, SUB), :] * factor
            forced = forced - s_ref[j] * factor
        pivot = jnp.broadcast_to(acc[0][k % SUB : k % SUB + 1, :], (SUB, LANES))
        scale = lax.rsqrt(pivot)
        scale = scale * (1.5 - 0.5 * pivot * scale * scale)
        for b in range(own, blocks):
            low_ref[pl.ds(offsets[k] - starts[k] + b * SUB, SUB), :] = acc[b - own] * scale
        forced = forced * scale
        s_ref[k] = forced
        for b in range(own + 1):
            inv[b] = inv[b] * scale
            inv_ref[k, pl.ds(b * SUB, SUB), :] = inv[b]
            mean[b] = mean[b] + inv[b] * forced
    for b in range(blocks):
        mean_ref[pl.ds(b * SUB, SUB), :] = mean[b]


def transforms(place, part, near, info, weight, fields):
    members, obs = ensemble(near)
    _, _, total = pair_rows(members)
    return call(
        functools.partial(transform_kernel, fields),
        [((members, members, LANES), F32), ((members, LANES), F32)],
        place,
        part,
        near,
        info,
        weight,
        scratch=gram_scratch(members, obs)
        + [
            pltpu.VMEM((total + members, LANES), F32),
            pltpu.VMEM((total, LANES), F32),
            pltpu.VMEM((members, SUB, LANES), F32),
        ],
    )


def apply_kernel(mems, k, place_ref, anomaly_ref, base_ref, inv_ref, *out_refs):
    members, rows, _ = anomaly_ref.shape
    memb_dev = members // (2 * mems)
    root = float(members - 1) ** 0.5
    blocks = rows // SUB
    if len(out_refs) == 1:
        out_refs = [out_refs[0].at[slot] for slot in range(2)]
    for slot in range(2):
        group = (place_ref[SECTION] ^ slot) * mems + (place_ref[MEM] ^ k)
        first = group * memb_dev
        zero = tuple(jnp.zeros((SUB, LANES), F32) for _ in range(memb_dev * blocks))

        def step(chunk, acc, first=first):
            acc = list(acc)
            for t in range(memb_dev):
                j = chunk * memb_dev + t
                fields = [anomaly_ref[j, pl.ds(b * SUB, SUB), :] for b in range(blocks)]
                for i in range(memb_dev):
                    factor = inv_ref[first + i, pl.ds(j, SUB, stride=0), :]
                    for b in range(blocks):
                        acc[i * blocks + b] = acc[i * blocks + b] + fields[b] * factor
            return tuple(acc)

        acc = lax.fori_loop(0, group + 1, step, zero)
        for i in range(memb_dev):
            for b in range(blocks):
                at = pl.ds(b * SUB, SUB)
                out_refs[slot][i, at, :] = base_ref[at, :] + root * acc[i * blocks + b]


def apply_transform(place, anomaly, base, inverse, mems, k, split):
    members, rows, width_y = anomaly.shape
    block = (members // (2 * mems), rows, width_y)
    outs = [(block, F32)] * 2 if split else [((2, *block), F32)]
    return call(functools.partial(apply_kernel, mems, k), outs, place, anomaly, base, inverse)


def unpack_kernel(share, mems, place_ref, *refs):
    near_refs, far_refs, (out_ref, all_ref, sem_ref) = refs[:mems], refs[mems : 2 * mems], refs[2 * mems :]
    memb_dev, total, _ = all_ref.shape
    levels = total // (2 * mems * share)
    width_x = total // levels
    copies = []
    for i in range(memb_dev):
        for other in range(2):
            for k in range(mems):
                group = (place_ref[SECTION] ^ other) * mems + (place_ref[MEM] ^ k)
                block_ref = (far_refs if other else near_refs)[k]
                if len(block_ref.shape) == 4:
                    block_ref = block_ref.at[other]
                for row in range(share):
                    all_ref[i, pl.ds(group * share + row, levels, stride=width_x), :] = block_ref[
                        i, pl.ds(row * levels, levels), :
                    ]
        copies.append(pltpu.make_async_copy(all_ref.at[i], out_ref.at[i], sem_ref.at[i]))
        copies[-1].start()
    for copy in copies:
        copy.wait()


def unpack(place, near, far, share, mems):
    memb_dev, rows, width_y = near[0].shape[-3:]
    vmem = pl.BlockSpec(memory_space=pltpu.VMEM)
    shape = (memb_dev, 2 * mems * rows, width_y)
    return pl.pallas_call(
        lambda *refs: unpack_kernel(share, mems, position(*place), *refs),
        in_specs=[vmem] * (2 * mems),
        out_specs=pl.BlockSpec(memory_space=pltpu.HBM),
        out_shape=jax.ShapeDtypeStruct(shape, F32),
        scratch_shapes=[pltpu.VMEM(shape, F32), pltpu.SemaphoreType.DMA((memb_dev,))],
        compiler_params=pltpu.CompilerParams(vmem_limit_bytes=VMEM_LIMIT),
        name="unpack",
    )(*[pltpu.with_memory_space_constraint(x, pltpu.VMEM) for x in (*near, *far)])


def along_tile(first, second):
    count = lax.axis_size("tile")

    def trade(value, start):
        pairs = []
        for i in range(start, count - 1, 2):
            pairs += [(i, i + 1), (i + 1, i)]
        return lax.ppermute(value, "tile", pairs)

    first = trade(first, 0)
    second = trade(second, 1)
    return first, second


def to_partner(value):
    return lax.ppermute(value, "section", [(0, 1), (1, 0)])


def over_mem(value, k):
    return lax.ppermute(value, "mem", [(i, i ^ k) for i in range(lax.axis_size("mem"))])


def across(value, k):
    size = lax.axis_size(GROUP)
    return lax.ppermute(value, GROUP, [(i, i ^ (size // 2) ^ k) for i in range(size)])


def analysis(state, speed_x, speed_y, diffuse, obs_cell, obs_value, obs_errinv, obs_list, obs_count):
    memb_dev, levels, width_x, _ = state.shape
    mems = lax.axis_size("mem")
    groups = lax.axis_size(GROUP)
    assert groups == 2 * mems and mems & (mems - 1) == 0
    tiles = lax.axis_size("tile")
    group_idx = lax.axis_index(GROUP)
    share = width_x // groups
    far = list(range(mems - 1, 0, -1))

    place = (tiles, width_x, share, mems)

    share_d = share // DB
    lists = lax.dynamic_slice_in_dim(obs_list, group_idx * share_d, share_d, 0)
    lists = lists.reshape(-1, obs_list.shape[2])
    counts = lax.dynamic_slice_in_dim(obs_count, group_idx * share_d, share_d, 0).reshape(-1, 1)

    a, b, info, fields, speed_x, speed_y, diffuse = pack(
        place, state, speed_x, speed_y, diffuse, obs_cell, obs_value, obs_errinv
    )
    fields = fields.reshape(state.shape)
    a, b = along_tile(a, b)
    inner = interior(place, fields, speed_x, speed_y, diffuse, obs_cell)
    keep, send, own_obs = forecast(
        place, fields, a, b, speed_x, speed_y, diffuse, obs_cell, inner, share, mems
    )

    other_obs = to_partner(own_obs)
    other = to_partner(send)
    both_obs = jnp.stack([own_obs, other_obs])
    gathered = [both_obs]
    for k in far[::-1]:
        gathered.append(over_mem(both_obs, k))
    gathered = jnp.stack(gathered)
    joined = join(place, keep, other)
    near = []
    for k in far[::-1]:
        near.append(over_mem(joined[k - 1], k))
    near_a, near_b = along_tile(gathered, gathered)
    weight = weights(place, lists, counts, info, a, b, memb_dev * levels)
    part = own_gram(place, gathered, info, weight)
    part = near_gram(place, part, near_a, a, weight, memb_dev * levels)
    inverse, mean = transforms(place, part, near_b, b, weight, memb_dev * levels)
    anomaly, base = centre(place, keep, other, near, mean)

    direct = None
    done, away = [None] * mems, [None] * mems
    for k in far + [0]:
        result = apply_transform(place, anomaly, base, inverse, mems, k, k == direct)
        done[k] = over_mem(result[0], k) if k else result[0]
        if k == direct:
            away[k] = across(result[1], k)
    for k in range(mems):
        if k != direct:
            away[k] = to_partner(done[k])
    return unpack(place, done, away, share, mems).reshape(state.shape)


def solution(mesh):
    placed = (
        P(GROUP, None, "tile", None),
        P(None, "tile", None),
        P(None, "tile", None),
        P("tile", None),
        P("tile"),
        P("tile"),
        P("tile"),
        P("tile", None, None),
        P("tile", None),
    )
    return jax.shard_map(
        analysis,
        mesh=mesh,
        in_specs=placed,
        out_specs=P(GROUP, None, "tile", None),
        check_vma=False,
    )
```
